32 devices in a mesh: replica: 8 (over z, core), shard: 4 (over y, x).
Axes of the slice: x: 2, y: 2, z: 4, core: 2. Of those that a mesh axis runs over, the one named last changes fastest.
Arguments:
- local_weights: bfloat16 [8, 8192, 512], P('replica', 'shard'), may hold values from -1.3258252 to 1.3258252
- outer_base: bfloat16 [8192, 512], P('shard'), may hold values from -0.0625 to 0.0625
- momentum: bfloat16 [8192, 512], P('shard', 'replica'), may hold values from -0.06591797 to 0.06591797
- error_feedback: bfloat16 [8, 8192, 512], P('replica', 'shard'), may hold values from -0.032958984 to 0.032958984
- q_start: float32 [512, 32], replicated, may hold values from -6 to 6
- tokens: bfloat16 [8, 512, 8192], P('replica', None, 'shard'), may hold values from -6 to 6
Outputs:
- new_base: bfloat16 [8192, 512], P('shard')
- new_momentum: bfloat16 [8192, 512], P('shard', 'replica')
- new_error: bfloat16 [8, 8192, 512], P('replica', 'shard')
- key_rows: bfloat16 [8, 512, 512], P('replica', 'shard')
The draws below stay inside these ranges and needn't reach their ends.
All inputs are finite; a program needn't handle non-finite values.
Results may differ from the reference program's by a relative error of at most 0.0065.
Values may be sent and summed in bfloat16 or wider, within the bound.
A program may use at most 64 MiB of HBM per device.

```python
import jax
import jax.numpy as jnp
from jax import lax

D = 8192
KV = 512
RANK = 32
TOKENS = 512
REPLICAS = 8


def draw_local_weights(key, part):
    key_noise = jax.random.fold_in(key, 11)
    key_rows = jax.random.fold_in(key, 12)
    key_cols = jax.random.fold_in(key, 13)
    noise_val = jax.random.normal(key_noise, (REPLICAS, D, KV), jnp.float32)
    noise_val = jnp.clip(noise_val, -4.0, 4.0)
    rise_rows = 3.0 ** (jnp.arange(D, dtype=jnp.float32) / D)
    row_spread = 10.0 ** jax.random.uniform(key_rows, (D,), jnp.float32)
    col_spread = 10.0 ** jax.random.uniform(key_cols, (KV,), jnp.float32)
    scaled = noise_val * (rise_rows * row_spread)[None, :, None] * col_spread[None, None, :]
    return (scaled * (0.1 * D ** (-0.5))).astype(jnp.bfloat16)


def shard_levels(stream_key, shape, pieces, smallest, largest):
    factor_of, own = 1.0, jax.random.fold_in(stream_key, 6)
    for axis_at, shards_of in pieces:
        heights = jnp.exp(jax.random.uniform(jax.random.fold_in(own, axis_at), (shards_of,), jnp.float32, smallest / len(pieces), largest / len(pieces)))
        factor_of = factor_of * jnp.repeat(heights, shape[axis_at] // shards_of).reshape([-1 if axis == axis_at else 1 for axis in range(len(shape))])
    return factor_of


def gaussian(own_key, dims, width, limit, pieces=(), kind=jnp.bfloat16):
    result = jax.random.normal(own_key, dims, jnp.float32) * width
    if len(pieces) > 0:
        result = shard_levels(own_key, dims, pieces, -0.22, 0.18) * result
    return jnp.clip(result, min=-limit, max=limit).astype(kind)


def setup_inputs(seed: int = 0) -> dict:
    key_list = jax.random.split(jax.random.key(seed), 7)
    return {
        "local_weights": draw_local_weights(jax.random.fold_in(key_list[6], 71), 0),
        "outer_base": gaussian(key_list[1], (D, KV), D ** -0.5, 0.0625, ((0, 4),)),
        "momentum": gaussian(key_list[2], (D, KV), (D ** -0.5), 0.06591797, ((0, 4), (1, 8))),
        "error_feedback": gaussian(key_list[3], (REPLICAS, D, KV), (0.5 * D ** -0.5), 0.032958984, ((0, 8), (1, 4))),
        "q_start": gaussian(key_list[4], (KV, RANK), 1.0, 6.0, (), jnp.float32),
        "tokens": gaussian(key_list[5], (REPLICAS, TOKENS, D), 1.0, 6.0, ((0, 8), (2, 4))),
    }


outer_mu = 0.9
outer_rate = 0.7

def reference(local_weights, outer_base, momentum, error_feedback, q_start, tokens):
    highest = lax.Precision.HIGHEST
    pseudo = outer_base.astype(jnp.float32)[None] - local_weights.astype(jnp.float32) + error_feedback.astype(jnp.float32)
    p_mean = jnp.einsum('rdk,kq->dq', pseudo, q_start, precision=highest) / REPLICAS
    gram = jnp.dot(p_mean.T, p_mean, precision=highest)
    factor_low = jnp.linalg.cholesky(gram)
    basis = jax.scipy.linalg.solve_triangular(factor_low, p_mean.T, lower=True).T
    q_mean = jnp.einsum('rdk,dq->kq', pseudo, basis, precision=highest) / REPLICAS
    update = jnp.dot(basis, q_mean.T, precision=highest)
    new_error = (pseudo - update[None]).astype(jnp.bfloat16)
    moment = outer_mu * momentum.astype(jnp.float32) + update
    new_base = (outer_base.astype(jnp.float32) - outer_rate * (outer_mu * moment + update)).astype(jnp.bfloat16)

    def project(token_block):
        return jnp.dot(token_block.astype(jnp.float32), new_base.astype(jnp.float32), preferred_element_type=jnp.float32).astype(jnp.bfloat16)
    key_rows = lax.map(project, tokens)
    return (new_base, moment.astype(jnp.bfloat16), new_error, key_rows)
```

```python
import functools

import jax
import jax.numpy as jnp
from jax import lax
from jax.experimental import pallas as pl
from jax.experimental.pallas import tpu as pltpu
from jax.sharding import PartitionSpec as P

outer_mu = 0.9
outer_rate = 0.7
MESH = pl.DeviceIdType.MESH
F32 = jnp.float32
BF16 = jnp.bfloat16
NT = (((1,), (1,)), ((), ()))
NN = (((1,), (0,)), ((), ()))
TN = (((0,), (0,)), ((), ()))
HIGHEST = lax.Precision.HIGHEST


def split3(x):
    high = x.astype(BF16)
    rest = x - high.astype(F32)
    mid = rest.astype(BF16)
    low = (rest - mid.astype(F32)).astype(BF16)
    return high, mid, low


def stack3(x):
    return jnp.concatenate(split3(x), axis=0)


def fold3(x):
    n = x.shape[0] // 3
    return x[:n] + (x[n : 2 * n] + x[2 * n :])


def invert(a):
    n = a.shape[0]
    rows = lax.broadcasted_iota(jnp.int32, (n, n), 0)
    cols = lax.broadcasted_iota(jnp.int32, (n, n), 1)
    lane = lax.broadcasted_iota(jnp.int32, (1, n), 1)
    for k in range(n):
        inverse_pivot = 1.0 / a[k : k + 1, k : k + 1]
        col = a[:, k : k + 1]
        row = jnp.where(lane == k, 1.0, a[k : k + 1, :]) * inverse_pivot
        a = jnp.where(rows == k, row, jnp.where(cols == k, 0.0, a) - col * row)
    return a


def exchange(cfg, lw, base, ef, qt, mom, pm_out, x_out, xo_out, slots,
             lw_v, base_v, ef_v, mom_v, pt, pair_in, half, rs_in, pm, gs, g_in,
             tl, tr_in, ts, ts_in, tt,
             ld_sem, mom_ld, pair_sem, rs_send, rs_recv, ag_send, ag_recv, fw_send,
             g_send, g_recv, tr_send, tr_recv, ts_send, ts_recv, ta_send, ta_recv,
             mr_send, ml_send, mf_send, m_recv, out_sem):
    R, S, d, kv, rank = cfg
    L = R // 2
    me = lax.axis_index("replica")
    shard = lax.axis_index("shard")
    core = lax.rem(me, 2)
    pos = me // 2
    partner = me + 1 - 2 * core
    chunks = ld_sem.shape[1]
    rows = d // chunks

    def at_replica(r):
        return {"replica": r}

    def at_shard(s):
        return {"shard": s}

    loads = []
    for k in range(chunks):
        trio = []
        for n, (src, dst) in enumerate(((lw, lw_v), (base, base_v), (ef, ef_v))):
            part = pl.ds(k * rows, rows)
            cp = pltpu.make_async_copy(src.at[part], dst.at[part], ld_sem.at[n, k])
            cp.start()
            trio.append(cp)
        loads.append(trio)
    own_in = pltpu.make_async_copy(mom, mom_v, mom_ld.at[0])
    own_in.start()

    barrier = pltpu.get_barrier_semaphore()
    for k in range(1, R):
        pl.semaphore_signal(barrier, inc=1, device_id=at_replica(lax.rem(me + k, R)), device_id_type=MESH)
    for k in range(1, S):
        pl.semaphore_signal(barrier, inc=1, device_id=at_shard(lax.rem(shard + k, S)), device_id_type=MESH)
    pl.semaphore_wait(barrier, R - 1 + S - 1)

    def rcopy(src, dst, ss, rs, dev):
        return pltpu.make_async_remote_copy(src_ref=src, dst_ref=dst, send_sem=ss, recv_sem=rs,
                                            device_id=dev, device_id_type=MESH)

    def block_of(p):
        return 2 * p + core

    def move(step, wait):
        right_origin = jnp.clip(pos - (step - 1), 0, L - 1)
        left_origin = jnp.clip(pos + (step - 1), 0, L - 1)

        def go(origin, sem, target):
            b = block_of(origin)
            src = mom_v if step == 1 else slots.at[b]
            cp = rcopy(src, slots.at[b], sem.at[step - 1], m_recv.at[b], at_replica(block_of(target)))
            cp.wait_send() if wait else cp.start()

        @pl.when((pos - (step - 1) >= 0) & (pos + 1 < L))
        def _():
            go(right_origin, mr_send, jnp.minimum(pos + 1, L - 1))

        @pl.when((pos + (step - 1) < L) & (pos >= 1))
        def _():
            go(left_origin, ml_send, jnp.maximum(pos - 1, 0))

    def forward(b, sem, src, wait):
        cp = rcopy(src, slots.at[b], sem, m_recv.at[b], at_replica(partner))
        cp.wait_send() if wait else cp.start()

    def arrived(step):
        for side, sign in enumerate((-1, 1)):
            origin = pos + sign * step

            @pl.when((origin >= 0) & (origin < L))
            def _():
                b = block_of(jnp.clip(origin, 0, L - 1))
                rcopy(slots.at[b], slots.at[b], mf_send.at[side, step - 1], m_recv.at[b], at_replica(partner)).wait_recv()
                forward(b, mf_send.at[side, step - 1], slots.at[b], False)

    own_in.wait()
    move(1, False)
    own_out = pltpu.make_async_copy(mom_v, slots.at[me], mom_ld.at[1])
    own_out.start()

    q3 = stack3(qt[...])
    for k in range(chunks):
        for cp in loads[k]:
            cp.wait()
        part = pl.ds(k * rows, rows)
        acc = lax.dot_general(q3, base_v[part, :], NT, preferred_element_type=F32)
        acc -= lax.dot_general(q3, lw_v[part, :], NT, preferred_element_type=F32)
        acc += lax.dot_general(q3, ef_v[part, :], NT, preferred_element_type=F32)
        pt[:, part] = fold3(acc)

    h = d // 2
    nc = L
    while h % nc or (h // nc) % 128:
        nc //= 2
    w = h // nc
    theirs = pl.ds(pl.multiple_of((1 - core) * h, 128), h)
    mine = pl.ds(pl.multiple_of(core * h, 128), h)
    pair = rcopy(pt.at[:, theirs], pair_in, pair_sem.at[0], pair_sem.at[1], at_replica(partner))
    pair.start()
    pair.wait_recv()
    half[...] = pt[:, mine] + pair_in[...]

    owner = pos < nc

    def when_owner(f):
        if nc == L:
            f()
        else:
            pl.when(owner)(f)

    def rs_copy(k):
        target = lax.rem(pos + k, L)
        src = half.at[:, pl.ds(pl.multiple_of(jnp.minimum(target, nc - 1) * w, 128), w)]
        return target, rcopy(src, rs_in.at[pos], rs_send.at[k], rs_recv.at[pos], at_replica(block_of(target)))

    def per_target(k, f):
        target, cp = rs_copy(k)
        if nc == L:
            f(cp)
        else:
            pl.when(target < nc)(lambda: f(cp))

    for k in range(1, L):
        per_target(k, lambda cp: cp.start())
    own_pos = jnp.minimum(pos, nc - 1)

    def cols_of(c, p):
        return pl.ds(pl.multiple_of(c * h + p * w, 128), w)

    def reduce_own():
        total = half[:, pl.ds(pl.multiple_of(own_pos * w, 128), w)]
        for k in range(1, L):
            source = lax.rem(pos + k, L)
            rcopy(rs_in.at[source], rs_in.at[source], rs_send.at[k], rs_recv.at[source], at_replica(partner)).wait_recv()
            total += rs_in[source]
        pm[:, cols_of(core, own_pos)] = total * (1.0 / R)
        for k in range(1, L):
            ag_copy(k).start()
        fw_copy(core, own_pos, fw_send.at[0]).start()

    def ag_copy(k):
        dst = pm.at[:, cols_of(core, own_pos)]
        return rcopy(dst, dst, ag_send.at[k], ag_recv.at[core, own_pos], at_replica(block_of(lax.rem(pos + k, L))))

    def fw_copy(c, p, sem):
        dst = pm.at[:, cols_of(c, p)]
        return rcopy(dst, dst, sem, ag_recv.at[c, p], at_replica(partner))

    when_owner(reduce_own)
    for k in range(1, L):
        source = lax.rem(pos + k, L)
        p = jnp.minimum(source, nc - 1)

        def take():
            fw_copy(core, p, fw_send.at[k]).wait_recv()
            fw_copy(core, p, fw_send.at[k]).start()

        if nc == L:
            take()
        else:
            pl.when(source < nc)(take)
    for p in range(nc):
        fw_copy(1 - core, p, fw_send.at[0]).wait_recv()

    whole_pm = pm[...]
    gs[...] = jnp.zeros_like(gs)
    gs[:, 0:rank] = lax.dot_general(whole_pm, whole_pm, NT, precision=HIGHEST, preferred_element_type=F32)

    def g_copy(k):
        return rcopy(gs, g_in.at[shard], g_send.at[k], g_recv.at[shard], at_shard(lax.rem(shard + k, S)))

    for k in range(1, S):
        g_copy(k).start()
    acc = None
    for k in range(chunks):
        part = pl.ds(k * rows, rows)
        p3 = stack3(pm[:, part])
        term = lax.dot_general(p3, base_v[part, :], NN, preferred_element_type=F32)
        term -= lax.dot_general(p3, lw_v[part, :], NN, preferred_element_type=F32)
        term += lax.dot_general(p3, ef_v[part, :], NN, preferred_element_type=F32)
        acc = term if acc is None else acc + term
    tl[...] = fold3(acc)

    groups = rank // 8
    tiles = min(R, groups * (kv // 128))
    wl = kv // (tiles // groups)

    def tile_of(j):
        return (pl.ds(pl.multiple_of(lax.rem(j, groups) * 8, 8), 8),
                pl.ds(pl.multiple_of((j // groups) * wl, 128), wl))

    t_owner = me < tiles

    def when_tile(cond, f):
        if tiles == R:
            f()
        else:
            pl.when(cond)(f)

    def tr_copy(k):
        target = lax.rem(me + k, R)
        a, b = tile_of(jnp.minimum(target, tiles - 1))
        return target < tiles, rcopy(tl.at[a, b], tr_in.at[me], tr_send.at[k], tr_recv.at[me], at_replica(target))

    for k in range(1, R):
        cond, cp = tr_copy(k)
        when_tile(cond, lambda cp=cp: cp.start())

    if L > 2:
        arrived(1)
        own_out.wait()
        move(2, False)
    elif L > 1:
        arrived(1)
        own_out.wait()
    else:
        own_out.wait()

    my_tile = tile_of(jnp.minimum(me, tiles - 1))

    def ts_copy(k):
        return rcopy(ts, ts_in.at[shard], ts_send.at[k], ts_recv.at[shard], at_shard(lax.rem(shard + k, S)))

    def ta_copy(k):
        dst = tt.at[my_tile[0], my_tile[1]]
        return rcopy(dst, dst, ta_send.at[k], ta_recv.at[jnp.minimum(me, tiles - 1)], at_replica(lax.rem(me + k, R)))

    def reduce_tile():
        total = tl[my_tile[0], my_tile[1]]
        for k in range(1, R):
            source = lax.rem(me + k, R)
            rcopy(tr_in.at[source], tr_in.at[source], tr_send.at[k], tr_recv.at[source], at_replica(partner)).wait_recv()
            total += tr_in[source]
        ts[...] = total
        for k in range(1, S):
            ts_copy(k).start()
        for k in range(1, S):
            source = lax.rem(shard + k, S)
            rcopy(ts_in.at[source], ts_in.at[source], ts_send.at[k], ts_recv.at[source], at_replica(partner)).wait_recv()
            total += ts_in[source]
        tt[my_tile[0], my_tile[1]] = total * (1.0 / R)
        for k in range(1, R):
            ta_copy(k).start()

    when_tile(t_owner, reduce_tile)

    for step in range(2, L):
        arrived(step)
        if step + 1 < L:
            move(step + 1, False)
    gram = gs[:, 0:rank]
    for k in range(1, S):
        source = lax.rem(shard + k, S)
        rcopy(g_in.at[source], g_in.at[source], g_send.at[k], g_recv.at[source], at_replica(partner)).wait_recv()
        gram = gram + g_in[source][:, 0:rank]
    inverse = invert(gram)

    for k in range(1, R):
        source = lax.rem(me + k, R)
        j = jnp.minimum(source, tiles - 1)
        a, b = tile_of(j)

        def got(j=j, a=a, b=b, k=k):
            rcopy(tt.at[a, b], tt.at[a, b], ta_send.at[k], ta_recv.at[j], at_replica(partner)).wait_recv()

        when_tile(source < tiles, got)
    x = lax.dot_general(inverse, tt[...], NN, precision=HIGHEST, preferred_element_type=F32)
    x_out[...] = x
    own_columns = xo_out.shape[1]
    pick = (lax.broadcasted_iota(jnp.int32, (kv, own_columns), 0)
            == me * own_columns + lax.broadcasted_iota(jnp.int32, (kv, own_columns), 1)).astype(F32)
    xo_out[...] = lax.dot_general(x, pick, NN, precision=HIGHEST, preferred_element_type=F32)
    pm_out[...] = whole_pm

    forward(me, mf_send.at[0, L - 1], mom_v, False)
    for p in range(L):
        b = 2 * p + 1 - core
        rcopy(slots.at[b], slots.at[b], mf_send.at[0, L - 1], m_recv.at[b], at_replica(partner)).wait_recv()

    forward(me, mf_send.at[0, L - 1], mom_v, True)
    pair.wait_send()
    for k in range(1, L):
        per_target(k, lambda cp: cp.wait_send())

    def drain_own():
        for k in range(1, L):
            ag_copy(k).wait_send()
        fw_copy(core, own_pos, fw_send.at[0]).wait_send()

    when_owner(drain_own)
    for k in range(1, L):
        source = lax.rem(pos + k, L)
        p = jnp.minimum(source, nc - 1)

        def drain_fw(p=p, k=k):
            fw_copy(core, p, fw_send.at[k]).wait_send()

        if nc == L:
            drain_fw()
        else:
            pl.when(source < nc)(drain_fw)
    for k in range(1, S):
        g_copy(k).wait_send()
    for k in range(1, R):
        cond, cp = tr_copy(k)
        when_tile(cond, lambda cp=cp: cp.wait_send())

    def drain_tile():
        for k in range(1, S):
            ts_copy(k).wait_send()
        for k in range(1, R):
            ta_copy(k).wait_send()

    when_tile(t_owner, drain_tile)
    for step in range(1, L):
        move(step, True)
        for side, sign in enumerate((-1, 1)):
            origin = pos + sign * step

            @pl.when((origin >= 0) & (origin < L))
            def _():
                b = block_of(jnp.clip(origin, 0, L - 1))
                forward(b, mf_send.at[side, step - 1], slots.at[b], True)


def local_step(tr, pm, x, xo, base, lw, ef, mom, slots, tokens,
               nb_out, nm_out, ne_out, kp_out, acc, x6, xo6):
    step = pl.program_id(0)

    def six_x(v):
        a, b, l = split3(v)
        return jnp.concatenate([a, b, a, l, b, a], axis=0)

    @pl.when(step == 0)
    def _():
        x6[...] = six_x(x[...])
        xo6[...] = six_x(xo[...])

    a, b, l = split3(pm[...])
    p6 = jnp.concatenate([a, a, b, a, b, l], axis=0)
    update = lax.dot_general(p6, x6[...], TN, preferred_element_type=F32)
    own_update = lax.dot_general(xo6[...], p6, TN, preferred_element_type=F32)
    nm_out[...] = (outer_mu * mom[...].astype(F32) + own_update).astype(BF16)
    base32 = base[...].astype(F32)
    ne_out[...] = ((base32 - lw[...].astype(F32) + ef[...].astype(F32)) - update).astype(BF16)
    full = slots[...].reshape(-1, tr).astype(F32).T
    moment = outer_mu * full + update
    nb = (base32 - outer_rate * (outer_mu * moment + update)).astype(BF16)
    nb_out[...] = nb
    term = jnp.dot(tokens[...], nb, preferred_element_type=F32)

    @pl.when(step == 0)
    def _():
        acc[...] = term

    @pl.when(step > 0)
    def _():
        acc[...] += term

    @pl.when(step == pl.num_programs(0) - 1)
    def _():
        kp_out[...] = acc[...].astype(BF16)


def key_scatter(S, kp, out, own, inbox, ld_sem, send, recv):
    shard = lax.axis_index("shard")
    n = out.shape[0]

    def part(s):
        return pl.ds(pl.multiple_of(s * n, 16), n)

    ld = pltpu.make_async_copy(kp.at[part(shard)], own, ld_sem)
    ld.start()
    barrier = pltpu.get_barrier_semaphore()
    for k in range(1, S):
        pl.semaphore_signal(barrier, inc=1, device_id={"shard": lax.rem(shard + k, S)}, device_id_type=MESH)
    pl.semaphore_wait(barrier, S - 1)

    def cp(k):
        target = lax.rem(shard + k, S)
        return pltpu.make_async_remote_copy(
            src_ref=kp.at[part(target)], dst_ref=inbox.at[shard], send_sem=send.at[k],
            recv_sem=recv.at[shard], device_id={"shard": target}, device_id_type=MESH)

    for k in range(1, S):
        cp(k).start()
    ld.wait()
    total = own[...].astype(F32)
    for k in range(1, S):
        source = lax.rem(shard + k, S)
        pltpu.make_async_remote_copy(
            src_ref=inbox.at[source], dst_ref=inbox.at[source], send_sem=send.at[k],
            recv_sem=recv.at[source], device_id={"shard": source}, device_id_type=MESH).wait_recv()
        total += inbox[source].astype(F32)
    out[...] = total.astype(BF16)
    for k in range(1, S):
        cp(k).wait_send()


def on_device(local_weights, outer_base, momentum, error_feedback, q_start, tokens):
    R = lax.axis_size("replica")
    S = lax.axis_size("shard")
    d, kv = outer_base.shape
    rank = q_start.shape[1]
    c = momentum.shape[1]
    L = R // 2
    lw, ef, tok = local_weights[0], error_feedback[0], tokens[0]
    nt = tok.shape[0]
    mom_t = momentum.T
    any_spec = pl.BlockSpec(memory_space=pl.ANY)
    vm = pl.BlockSpec(memory_space=pltpu.VMEM)
    chunks = min(4, d // 128)
    h = d // 2
    nc = L
    while h % nc or (h // nc) % 128:
        nc //= 2
    w = h // nc
    tiles = min(R, (rank // 8) * (kv // 128))
    wl = kv // (tiles // (rank // 8))
    V = pltpu.VMEM
    dma = pltpu.SemaphoreType.DMA
    pm, x, xo, slots = pl.pallas_call(
        functools.partial(exchange, (R, S, d, kv, rank)),
        out_shape=(
            jax.ShapeDtypeStruct((rank, d), F32),
            jax.ShapeDtypeStruct((rank, kv), F32),
            jax.ShapeDtypeStruct((rank, c), F32),
            jax.ShapeDtypeStruct((R, c, d), BF16),
        ),
        in_specs=[any_spec, any_spec, any_spec, vm, any_spec],
        out_specs=(vm, vm, vm, any_spec),
        scratch_shapes=[
            V((d, kv), BF16), V((d, kv), BF16), V((d, kv), BF16), V((c, d), BF16),
            V((rank, d), F32), V((rank, h), F32), V((rank, h), F32), V((L, rank, w), F32), V((rank, d), F32),
            V((rank, 128), F32), V((S, rank, 128), F32),
            V((rank, kv), F32), V((R, 8, wl), F32), V((8, wl), F32), V((S, 8, wl), F32), V((rank, kv), F32),
            dma((3, chunks)), dma((2,)), dma((2,)), dma((L,)), dma((L,)), dma((L,)), dma((2, L)), dma((L,)),
            dma((S,)), dma((S,)), dma((R,)), dma((R,)), dma((S,)), dma((S,)), dma((R,)), dma((R,)),
            dma((L,)), dma((L,)), dma((2, L)), dma((R,)), dma((1,)),
        ],
        compiler_params=pltpu.CompilerParams(collective_id=0, has_side_effects=True),
        name="exchange",
    )(lw, outer_base, ef, q_start.T, mom_t)

    tr = 256
    row = lambda i: (i, 0)
    nb, nm, ne, kp = pl.pallas_call(
        functools.partial(local_step, tr),
        grid=(d // tr,),
        out_shape=(
            jax.ShapeDtypeStruct((d, kv), BF16),
            jax.ShapeDtypeStruct((c, d), BF16),
            jax.ShapeDtypeStruct((d, kv), BF16),
            jax.ShapeDtypeStruct((nt, kv), BF16),
        ),
        in_specs=[
            pl.BlockSpec((rank, tr), lambda i: (0, i)),
            pl.BlockSpec((rank, kv), lambda i: (0, 0)),
            pl.BlockSpec((rank, c), lambda i: (0, 0)),
            pl.BlockSpec((tr, kv), row),
            pl.BlockSpec((tr, kv), row),
            pl.BlockSpec((tr, kv), row),
            pl.BlockSpec((c, tr), lambda i: (0, i)),
            pl.BlockSpec((R, c, tr), lambda i: (0, 0, i)),
            pl.BlockSpec((nt, tr), lambda i: (0, i)),
        ],
        out_specs=(
            pl.BlockSpec((tr, kv), row),
            pl.BlockSpec((c, tr), lambda i: (0, i)),
            pl.BlockSpec((tr, kv), row),
            pl.BlockSpec((nt, kv), lambda i: (0, 0)),
        ),
        scratch_shapes=[V((nt, kv), F32), V((6 * rank, kv), BF16), V((6 * rank, c), BF16)],
        compiler_params=pltpu.CompilerParams(dimension_semantics=("arbitrary",)),
        name="local_step",
    )(pm, x, xo, outer_base, lw, ef, mom_t, slots, tok)

    n = nt // S
    keys = pl.pallas_call(
        functools.partial(key_scatter, S),
        out_shape=jax.ShapeDtypeStruct((n, kv), BF16),
        in_specs=[any_spec],
        out_specs=vm,
        scratch_shapes=[V((n, kv), BF16), V((S, n, kv), BF16), dma(()), dma((S,)), dma((S,))],
        compiler_params=pltpu.CompilerParams(collective_id=1, has_side_effects=True),
        name="key_scatter",
    )(kp)
    return nb, nm.T, ne[None], keys[None]


def solution(mesh):
    in_specs = (
        P("replica", "shard", None),
        P("shard", None),
        P("shard", "replica"),
        P("replica", "shard", None),
        P(),
        P("replica", None, "shard"),
    )
    out_specs = (
        P("shard", None),
        P("shard", "replica"),
        P("replica", "shard", None),
        P("replica", "shard", None),
    )
    return jax.shard_map(
        on_device, mesh=mesh, in_specs=in_specs, out_specs=out_specs, check_vma=False
    )
```

```python
import functools

import jax
import jax.numpy as jnp
from jax import lax
from jax.experimental import pallas as pl
from jax.experimental.pallas import tpu as pltpu
from jax.sharding import PartitionSpec as P

outer_mu = 0.9
outer_rate = 0.7
MESH = pl.DeviceIdType.MESH
F32 = jnp.float32
BF16 = jnp.bfloat16
NT = (((1,), (1,)), ((), ()))
NN = (((1,), (0,)), ((), ()))
TN = (((0,), (0,)), ((), ()))
HIGHEST = lax.Precision.HIGHEST


def split3(x):
    high = x.astype(BF16)
    rest = x - high.astype(F32)
    mid = rest.astype(BF16)
    low = (rest - mid.astype(F32)).astype(BF16)
    return high, mid, low


def stack3(x):
    return jnp.concatenate(split3(x), axis=0)


def fold3(x):
    n = x.shape[0] // 3
    return x[:n] + (x[n : 2 * n] + x[2 * n :])


def invert(a):
    n = a.shape[0]
    rows = lax.broadcasted_iota(jnp.int32, (n, n), 0)
    cols = lax.broadcasted_iota(jnp.int32, (n, n), 1)
    lane = lax.broadcasted_iota(jnp.int32, (1, n), 1)
    for k in range(n):
        inverse_pivot = 1.0 / a[k : k + 1, k : k + 1]
        col = a[:, k : k + 1]
        row = jnp.where(lane == k, 1.0, a[k : k + 1, :]) * inverse_pivot
        a = jnp.where(rows == k, row, jnp.where(cols == k, 0.0, a) - col * row)
    return a


def exchange(cfg, lw, base, ef, qt, mom, tok, pm_out, x_out, xo_out, a_out, b_out, mom_out,
             lw_v, base_v, ef_v, tok_v, slots, mom_rows, pt, pair_in, half, rs_in, pm, gs, g_in,
             tl, tr_in, ts, ts_in, tt,
             ld_sem, mom_ld, pair_sem, rs_send, rs_recv, ag_send, ag_recv, fw_send,
             g_send, g_recv, tr_send, tr_recv, ts_send, ts_recv, ta_send, ta_recv,
             mr_send, ml_send, mf_send, m_recv, out_sem,
             a_buf, a_bf, a_in, bt, b_in, a_send, a_recv, b_send, b_recv):
    R, S, d, kv, rank = cfg
    L = R // 2
    me = lax.axis_index("replica")
    shard = lax.axis_index("shard")
    core = lax.rem(me, 2)
    pos = me // 2
    partner = me + 1 - 2 * core
    chunks = ld_sem.shape[1]
    rows = d // chunks

    def at_replica(r):
        return {"replica": r}

    def at_shard(s):
        return {"shard": s}

    loads = []
    for k in range(chunks):
        trio = []
        for n, (src, dst) in enumerate(((lw, lw_v), (base, base_v), (ef, ef_v))):
            part = pl.ds(k * rows, rows)
            cp = pltpu.make_async_copy(src.at[part], dst.at[part], ld_sem.at[n, k])
            cp.start()
            trio.append(cp)
        loads.append(trio)
    own_in = pltpu.make_async_copy(mom, slots.at[me], mom_ld.at[0])
    own_in.start()
    tok_in = pltpu.make_async_copy(tok, tok_v, mom_ld.at[1])
    tok_in.start()

    barrier = pltpu.get_barrier_semaphore()
    for k in range(1, R):
        pl.semaphore_signal(barrier, inc=1, device_id=at_replica(lax.rem(me + k, R)), device_id_type=MESH)
    for k in range(1, S):
        pl.semaphore_signal(barrier, inc=1, device_id=at_shard(lax.rem(shard + k, S)), device_id_type=MESH)
    pl.semaphore_wait(barrier, R - 1 + S - 1)

    def rcopy(src, dst, ss, rs, dev):
        return pltpu.make_async_remote_copy(src_ref=src, dst_ref=dst, send_sem=ss, recv_sem=rs,
                                            device_id=dev, device_id_type=MESH)

    def block_of(p):
        return 2 * p + core

    def move(step, wait):
        right_origin = jnp.clip(pos - (step - 1), 0, L - 1)
        left_origin = jnp.clip(pos + (step - 1), 0, L - 1)

        def go(origin, sem, target):
            b = block_of(origin)
            cp = rcopy(slots.at[b], slots.at[b], sem.at[step - 1], m_recv.at[b], at_replica(block_of(target)))
            cp.wait_send() if wait else cp.start()

        @pl.when((pos - (step - 1) >= 0) & (pos + 1 < L))
        def _():
            go(right_origin, mr_send, jnp.minimum(pos + 1, L - 1))

        @pl.when((pos + (step - 1) < L) & (pos >= 1))
        def _():
            go(left_origin, ml_send, jnp.maximum(pos - 1, 0))

    def forward(b, sem, src, wait):
        cp = rcopy(src, slots.at[b], sem, m_recv.at[b], at_replica(partner))
        cp.wait_send() if wait else cp.start()

    def arrived(step):
        for side, sign in enumerate((-1, 1)):
            origin = pos + sign * step

            @pl.when((origin >= 0) & (origin < L))
            def _():
                b = block_of(jnp.clip(origin, 0, L - 1))
                rcopy(slots.at[b], slots.at[b], mf_send.at[side, step - 1], m_recv.at[b], at_replica(partner)).wait_recv()
                forward(b, mf_send.at[side, step - 1], slots.at[b], False)

    own_in.wait()
    move(1, False)
    forward(me, mf_send.at[0, L - 1], slots.at[me], False)

    c = slots.shape[1]
    per = 128 // c
    blocks = kv // 128
    n = tok.shape[0] // S
    early = per == 2

    def token_rows(s):
        return pl.ds(pl.multiple_of(s * n, 128), n)

    def block_cols(bk):
        return pl.ds(pl.multiple_of(bk * 128, 128), 128)

    def a_copy(k, bk):
        target = lax.rem(shard + k, S)
        return rcopy(a_bf.at[token_rows(target), block_cols(bk)], a_in.at[shard, :, block_cols(bk)],
                     a_send.at[k, bk], a_recv.at[shard, bk], at_shard(target))

    def mom_copy(bk):
        return pltpu.make_async_copy(mom_rows.at[:, block_cols(bk)], mom_out.at[:, block_cols(bk)], out_sem.at[bk])

    def key_block(bk):
        cols = block_cols(bk)
        block = slots[pl.ds(bk * per, per)].reshape(128, d)
        a = a_buf[:, cols] - (outer_rate * outer_mu * outer_mu) * lax.dot_general(
            tok_v[...], block, NT, preferred_element_type=F32)
        a_buf[:, cols] = a
        a_bf[:, cols] = a.astype(BF16)
        for k in range(1, S):
            a_copy(k, bk).start()
        mom_rows[:, cols] = block.T
        mom_copy(bk).start()

    def partner_block(p):
        b = 2 * p + 1 - core
        rcopy(slots.at[b], slots.at[b], mf_send.at[0, L - 1], m_recv.at[b], at_replica(partner)).wait_recv()

    def blocks_at(step):
        def side(i, carry):
            origin = pos + (2 * i - 1) * step

            @pl.when((origin >= 0) & (origin < L))
            def _():
                p = jnp.clip(origin, 0, L - 1)
                partner_block(p)
                if early:
                    key_block(p)

            return carry

        lax.fori_loop(0, 2, side, 0)

    q3 = stack3(qt[...])
    for k in range(chunks):
        for cp in loads[k]:
            cp.wait()
        part = pl.ds(k * rows, rows)
        acc = lax.dot_general(q3, base_v[part, :], NT, preferred_element_type=F32)
        acc -= lax.dot_general(q3, lw_v[part, :], NT, preferred_element_type=F32)
        acc += lax.dot_general(q3, ef_v[part, :], NT, preferred_element_type=F32)
        pt[:, part] = fold3(acc)

    h = d // 2
    nc = L
    while h % nc or (h // nc) % 128:
        nc //= 2
    w = h // nc
    theirs = pl.ds(pl.multiple_of((1 - core) * h, 128), h)
    mine = pl.ds(pl.multiple_of(core * h, 128), h)
    pair = rcopy(pt.at[:, theirs], pair_in, pair_sem.at[0], pair_sem.at[1], at_replica(partner))
    pair.start()
    tok_in.wait()
    a_buf[...] = jnp.dot(tok_v[...], base_v[...], preferred_element_type=F32)
    pair.wait_recv()
    half[...] = pt[:, mine] + pair_in[...]

    owner = pos < nc

    def when_owner(f):
        if nc == L:
            f()
        else:
            pl.when(owner)(f)

    def rs_copy(k):
        target = lax.rem(pos + k, L)
        src = half.at[:, pl.ds(pl.multiple_of(jnp.minimum(target, nc - 1) * w, 128), w)]
        return target, rcopy(src, rs_in.at[pos], rs_send.at[k], rs_recv.at[pos], at_replica(block_of(target)))

    def per_target(k, f):
        target, cp = rs_copy(k)
        if nc == L:
            f(cp)
        else:
            pl.when(target < nc)(lambda: f(cp))

    for k in range(1, L):
        per_target(k, lambda cp: cp.start())
    partner_block(pos)
    if early:
        key_block(pos)
    own_pos = jnp.minimum(pos, nc - 1)

    def cols_of(c, p):
        return pl.ds(pl.multiple_of(c * h + p * w, 128), w)

    def reduce_own():
        total = half[:, pl.ds(pl.multiple_of(own_pos * w, 128), w)]
        for k in range(1, L):
            source = lax.rem(pos + k, L)
            rcopy(rs_in.at[source], rs_in.at[source], rs_send.at[k], rs_recv.at[source], at_replica(partner)).wait_recv()
            total += rs_in[source]
        pm[:, cols_of(core, own_pos)] = total * (1.0 / R)
        for k in range(1, L):
            ag_copy(k).start()
        fw_copy(core, own_pos, fw_send.at[0]).start()

    def ag_copy(k):
        dst = pm.at[:, cols_of(core, own_pos)]
        return rcopy(dst, dst, ag_send.at[k], ag_recv.at[core, own_pos], at_replica(block_of(lax.rem(pos + k, L))))

    def fw_copy(c, p, sem):
        dst = pm.at[:, cols_of(c, p)]
        return rcopy(dst, dst, sem, ag_recv.at[c, p], at_replica(partner))

    when_owner(reduce_own)
    if L > 1:
        arrived(1)
    for k in range(1, L):
        source = lax.rem(pos + k, L)
        p = jnp.minimum(source, nc - 1)

        def take():
            fw_copy(core, p, fw_send.at[k]).wait_recv()
            fw_copy(core, p, fw_send.at[k]).start()

        if nc == L:
            take()
        else:
            pl.when(source < nc)(take)
    for p in range(nc):
        fw_copy(1 - core, p, fw_send.at[0]).wait_recv()

    acc = None
    for k in range(chunks):
        part = pl.ds(k * rows, rows)
        p3 = stack3(pm[:, part])
        term = lax.dot_general(p3, base_v[part, :], NN, preferred_element_type=F32)
        term -= lax.dot_general(p3, lw_v[part, :], NN, preferred_element_type=F32)
        term += lax.dot_general(p3, ef_v[part, :], NN, preferred_element_type=F32)
        acc = term if acc is None else acc + term
    tl[...] = fold3(acc)

    groups = rank // 8
    tiles = min(R, groups * (kv // 128))
    wl = kv // (tiles // groups)

    def tile_of(j):
        return (pl.ds(pl.multiple_of(lax.rem(j, groups) * 8, 8), 8),
                pl.ds(pl.multiple_of((j // groups) * wl, 128), wl))

    t_owner = me < tiles

    def when_tile(cond, f):
        if tiles == R:
            f()
        else:
            pl.when(cond)(f)

    def tr_copy(k):
        target = lax.rem(me + k, R)
        a, b = tile_of(jnp.minimum(target, tiles - 1))
        return target < tiles, rcopy(tl.at[a, b], tr_in.at[me], tr_send.at[k], tr_recv.at[me], at_replica(target))

    for k in range(1, R):
        cond, cp = tr_copy(k)
        when_tile(cond, lambda cp=cp: cp.start())

    if L > 2:
        move(2, False)

    whole_pm = pm[...]
    gs[...] = jnp.zeros_like(gs)
    gs[:, 0:rank] = lax.dot_general(whole_pm, whole_pm, NT, precision=HIGHEST, preferred_element_type=F32)

    def g_copy(k):
        return rcopy(gs, g_in.at[shard], g_send.at[k], g_recv.at[shard], at_shard(lax.rem(shard + k, S)))

    for k in range(1, S):
        g_copy(k).start()
    b_acc = None
    for k in range(chunks):
        part = pl.ds(k * rows, rows)
        term = lax.dot_general(stack3(pm[:, part]), tok_v[:, part], NT, preferred_element_type=F32)
        b_acc = term if b_acc is None else b_acc + term
    bt[...] = fold3(b_acc)

    def b_copy(k):
        target = lax.rem(shard + k, S)
        return rcopy(bt.at[:, token_rows(target)], b_in.at[shard], b_send.at[k], b_recv.at[shard], at_shard(target))

    for k in range(1, S):
        b_copy(k).start()

    my_tile = tile_of(jnp.minimum(me, tiles - 1))

    def ts_copy(k):
        return rcopy(ts, ts_in.at[shard], ts_send.at[k], ts_recv.at[shard], at_shard(lax.rem(shard + k, S)))

    def ta_copy(k):
        dst = tt.at[my_tile[0], my_tile[1]]
        return rcopy(dst, dst, ta_send.at[k], ta_recv.at[jnp.minimum(me, tiles - 1)], at_replica(lax.rem(me + k, R)))

    def reduce_replicas():
        total = tl[my_tile[0], my_tile[1]]
        for k in range(1, R):
            source = lax.rem(me + k, R)
            rcopy(tr_in.at[source], tr_in.at[source], tr_send.at[k], tr_recv.at[source], at_replica(partner)).wait_recv()
            total += tr_in[source]
        ts[...] = total
        for k in range(1, S):
            ts_copy(k).start()

    def reduce_shards():
        total = ts[...]
        for k in range(1, S):
            source = lax.rem(shard + k, S)
            rcopy(ts_in.at[source], ts_in.at[source], ts_send.at[k], ts_recv.at[source], at_replica(partner)).wait_recv()
            total += ts_in[source]
        tt[my_tile[0], my_tile[1]] = total * (1.0 / R)
        for k in range(1, R):
            ta_copy(k).start()

    when_tile(t_owner, reduce_replicas)
    if L > 1:
        blocks_at(1)
    when_tile(t_owner, reduce_shards)

    if L > 2:
        arrived(2)
        if L > 3:
            move(3, False)

    gram = gs[:, 0:rank]
    for k in range(1, S):
        source = lax.rem(shard + k, S)
        rcopy(g_in.at[source], g_in.at[source], g_send.at[k], g_recv.at[source], at_replica(partner)).wait_recv()
        gram = gram + g_in[source][:, 0:rank]
    inverse = invert(gram)
    for step in range(2, L):
        if step > 2:
            arrived(step)
            if step + 1 < L:
                move(step + 1, False)
        if step < L - 1:
            blocks_at(step)

    for k in range(1, R):
        source = lax.rem(me + k, R)
        j = jnp.minimum(source, tiles - 1)
        a, b = tile_of(j)

        def got(j=j, a=a, b=b, k=k):
            rcopy(tt.at[a, b], tt.at[a, b], ta_send.at[k], ta_recv.at[j], at_replica(partner)).wait_recv()

        when_tile(source < tiles, got)
    x = lax.dot_general(inverse, tt[...], NN, precision=HIGHEST, preferred_element_type=F32)
    x_out[...] = x
    own_columns = xo_out.shape[1]
    pick = (lax.broadcasted_iota(jnp.int32, (kv, own_columns), 0)
            == me * own_columns + lax.broadcasted_iota(jnp.int32, (kv, own_columns), 1)).astype(F32)
    xo_out[...] = lax.dot_general(x, pick, NN, precision=HIGHEST, preferred_element_type=F32)
    pm_out[...] = pm[...]

    if L > 2:
        blocks_at(L - 1)
    if not early:
        def late(bk, carry):
            key_block(bk)
            return carry

        lax.fori_loop(0, blocks, late, 0)

    total = a_buf[token_rows(shard), :]
    b_total = bt[:, token_rows(shard)]
    for k in range(1, S):
        source = lax.rem(shard + k, S)
        for bk in range(blocks):
            part = a_in.at[source, :, block_cols(bk)]
            rcopy(part, part, a_send.at[k, bk], a_recv.at[source, bk], at_replica(partner)).wait_recv()
        total += a_in[source].astype(F32)
        rcopy(b_in.at[source], b_in.at[source], b_send.at[k], b_recv.at[source], at_replica(partner)).wait_recv()
        b_total += b_in[source]
    a_out[...] = total
    b_out[...] = b_total
    for bk in range(blocks):
        mom_copy(bk).wait()

    forward(me, mf_send.at[0, L - 1], slots.at[me], True)
    for k in range(1, S):
        for bk in range(blocks):
            a_copy(k, bk).wait_send()
        b_copy(k).wait_send()
    pair.wait_send()
    for k in range(1, L):
        per_target(k, lambda cp: cp.wait_send())

    def drain_own():
        for k in range(1, L):
            ag_copy(k).wait_send()
        fw_copy(core, own_pos, fw_send.at[0]).wait_send()

    when_owner(drain_own)
    for k in range(1, L):
        source = lax.rem(pos + k, L)
        p = jnp.minimum(source, nc - 1)

        def drain_fw(p=p, k=k):
            fw_copy(core, p, fw_send.at[k]).wait_send()

        if nc == L:
            drain_fw()
        else:
            pl.when(source < nc)(drain_fw)
    for k in range(1, S):
        g_copy(k).wait_send()
    for k in range(1, R):
        cond, cp = tr_copy(k)
        when_tile(cond, lambda cp=cp: cp.wait_send())

    def drain_tile():
        for k in range(1, S):
            ts_copy(k).wait_send()
        for k in range(1, R):
            ta_copy(k).wait_send()

    when_tile(t_owner, drain_tile)
    for step in range(1, L):
        move(step, True)
        for side, sign in enumerate((-1, 1)):
            origin = pos + sign * step

            @pl.when((origin >= 0) & (origin < L))
            def _():
                b = block_of(jnp.clip(origin, 0, L - 1))
                forward(b, mf_send.at[side, step - 1], slots.at[b], True)


def local_step(tr, pm, x, xo, a_own, b_own, base, lw, ef, mom, mom_rows,
               nb_out, nm_out, ne_out, key_out, x6, xo6):
    step = pl.program_id(0)

    def six_x(v):
        a, b, l = split3(v)
        return jnp.concatenate([a, b, a, l, b, a], axis=0)

    @pl.when(step == 0)
    def _():
        x6[...] = six_x(x[...])
        xo6[...] = six_x(xo[...])
        key_out[...] = (a_own[...] - (outer_rate * (outer_mu + 1.0)) * lax.dot_general(
            b_own[...], x[...], TN, precision=HIGHEST, preferred_element_type=F32)).astype(BF16)

    a, b, l = split3(pm[...])
    p6 = jnp.concatenate([a, a, b, a, b, l], axis=0)
    update = lax.dot_general(p6, x6[...], TN, preferred_element_type=F32)
    own_update = lax.dot_general(xo6[...], p6, TN, preferred_element_type=F32)
    nm_out[...] = (outer_mu * mom[...].astype(F32) + own_update).astype(BF16)
    base32 = base[...].astype(F32)
    ne_out[...] = ((base32 - lw[...].astype(F32) + ef[...].astype(F32)) - update).astype(BF16)
    moment = outer_mu * mom_rows[...].astype(F32) + update
    nb_out[...] = (base32 - outer_rate * (outer_mu * moment + update)).astype(BF16)


def on_device(local_weights, outer_base, momentum, error_feedback, q_start, tokens):
    R = lax.axis_size("replica")
    S = lax.axis_size("shard")
    d, kv = outer_base.shape
    rank = q_start.shape[1]
    c = momentum.shape[1]
    L = R // 2
    lw, ef, tok = local_weights[0], error_feedback[0], tokens[0]
    nt = tok.shape[0]
    mom_t = momentum.T
    any_spec = pl.BlockSpec(memory_space=pl.ANY)
    vm = pl.BlockSpec(memory_space=pltpu.VMEM)
    chunks = min(4, d // 128)
    h = d // 2
    nc = L
    while h % nc or (h // nc) % 128:
        nc //= 2
    w = h // nc
    tiles = min(R, (rank // 8) * (kv // 128))
    wl = kv // (tiles // (rank // 8))
    V = pltpu.VMEM
    dma = pltpu.SemaphoreType.DMA
    n = nt // S
    pm, x, xo, a_own, b_own, mom_rows = pl.pallas_call(
        functools.partial(exchange, (R, S, d, kv, rank)),
        out_shape=(
            jax.ShapeDtypeStruct((rank, d), F32),
            jax.ShapeDtypeStruct((rank, kv), F32),
            jax.ShapeDtypeStruct((rank, c), F32),
            jax.ShapeDtypeStruct((n, kv), F32),
            jax.ShapeDtypeStruct((rank, n), F32),
            jax.ShapeDtypeStruct((d, kv), BF16),
        ),
        in_specs=[any_spec, any_spec, any_spec, vm, any_spec, any_spec],
        out_specs=(vm, vm, vm, vm, vm, any_spec),
        scratch_shapes=[
            V((d, kv), BF16), V((d, kv), BF16), V((d, kv), BF16), V((nt, d), BF16), V((R, c, d), BF16), V((d, kv), BF16),
            V((rank, d), F32), V((rank, h), F32), V((rank, h), F32), V((L, rank, w), F32), V((rank, d), F32),
            V((rank, 128), F32), V((S, rank, 128), F32),
            V((rank, kv), F32), V((R, 8, wl), F32), V((8, wl), F32), V((S, 8, wl), F32), V((rank, kv), F32),
            dma((3, chunks)), dma((2,)), dma((2,)), dma((L,)), dma((L,)), dma((L,)), dma((2, L)), dma((L,)),
            dma((S,)), dma((S,)), dma((R,)), dma((R,)), dma((S,)), dma((S,)), dma((R,)), dma((R,)),
            dma((L,)), dma((L,)), dma((2, L)), dma((R,)), dma((kv // 128,)),
            V((nt, kv), F32), V((nt, kv), BF16), V((S, n, kv), BF16), V((rank, nt), F32), V((S, rank, n), F32),
            dma((S, kv // 128)), dma((S, kv // 128)), dma((S,)), dma((S,)),
        ],
        compiler_params=pltpu.CompilerParams(collective_id=0, has_side_effects=True),
        name="exchange",
    )(lw, outer_base, ef, q_start.T, mom_t, tok)

    tr = 256
    row = lambda i: (i, 0)
    nb, nm, ne, keys = pl.pallas_call(
        functools.partial(local_step, tr),
        grid=(d // tr,),
        out_shape=(
            jax.ShapeDtypeStruct((d, kv), BF16),
            jax.ShapeDtypeStruct((c, d), BF16),
            jax.ShapeDtypeStruct((d, kv), BF16),
            jax.ShapeDtypeStruct((n, kv), BF16),
        ),
        in_specs=[
            pl.BlockSpec((rank, tr), lambda i: (0, i)),
            pl.BlockSpec((rank, kv), lambda i: (0, 0)),
            pl.BlockSpec((rank, c), lambda i: (0, 0)),
            pl.BlockSpec((n, kv), lambda i: (0, 0)),
            pl.BlockSpec((rank, n), lambda i: (0, 0)),
            pl.BlockSpec((tr, kv), row),
            pl.BlockSpec((tr, kv), row),
            pl.BlockSpec((tr, kv), row),
            pl.BlockSpec((c, tr), lambda i: (0, i)),
            pl.BlockSpec((tr, kv), row),
        ],
        out_specs=(
            pl.BlockSpec((tr, kv), row),
            pl.BlockSpec((c, tr), lambda i: (0, i)),
            pl.BlockSpec((tr, kv), row),
            pl.BlockSpec((n, kv), lambda i: (0, 0)),
        ),
        scratch_shapes=[V((6 * rank, kv), BF16), V((6 * rank, c), BF16)],
        compiler_params=pltpu.CompilerParams(dimension_semantics=("arbitrary",)),
        name="local_step",
    )(pm, x, xo, a_own, b_own, outer_base, lw, ef, mom_t, mom_rows)

    return nb, nm.T, ne[None], keys[None]


def solution(mesh):
    in_specs = (
        P("replica", "shard", None),
        P("shard", None),
        P("shard", "replica"),
        P("replica", "shard", None),
        P(),
        P("replica", None, "shard"),
    )
    out_specs = (
        P("shard", None),
        P("shard", "replica"),
        P("replica", "shard", None),
        P("replica", "shard", None),
    )
    return jax.shard_map(
        on_device, mesh=mesh, in_specs=in_specs, out_specs=out_specs, check_vma=False
    )
```

```python
import functools

import jax
import jax.numpy as jnp
from jax import lax
from jax.experimental import pallas as pl
from jax.experimental.pallas import tpu as pltpu
from jax.sharding import PartitionSpec as P

outer_mu = 0.9
outer_rate = 0.7
MESH = pl.DeviceIdType.MESH
F32 = jnp.float32
BF16 = jnp.bfloat16
NT = (((1,), (1,)), ((), ()))
NN = (((1,), (0,)), ((), ()))
TN = (((0,), (0,)), ((), ()))
HIGHEST = lax.Precision.HIGHEST


def split3(x):
    high = x.astype(BF16)
    rest = x - high.astype(F32)
    mid = rest.astype(BF16)
    low = (rest - mid.astype(F32)).astype(BF16)
    return high, mid, low


def stack3(x):
    return jnp.concatenate(split3(x), axis=0)


def fold3(x):
    n = x.shape[0] // 3
    return x[:n] + (x[n : 2 * n] + x[2 * n :])


def invert(a):
    n = a.shape[0]
    rows = lax.broadcasted_iota(jnp.int32, (n, n), 0)
    cols = lax.broadcasted_iota(jnp.int32, (n, n), 1)
    lane = lax.broadcasted_iota(jnp.int32, (1, n), 1)
    for k in range(n):
        inverse_pivot = 1.0 / a[k : k + 1, k : k + 1]
        col = a[:, k : k + 1]
        row = jnp.where(lane == k, 1.0, a[k : k + 1, :]) * inverse_pivot
        a = jnp.where(rows == k, row, jnp.where(cols == k, 0.0, a) - col * row)
    return a


def exchange(cfg, lw, base, ef, qt, mom, tok, pm_out, x_out, xo_out, a_out, b_out, mom_out,
             lw_v, base_v, ef_v, tok_v, slots, mom_rows, pt, pair_in, half, rs_in, pm, gs, g_in,
             tl, tr_in, ts, ts_in, tt,
             ld_sem, mom_ld, pair_sem, rs_send, rs_recv, ag_send, ag_recv, fw_send,
             g_send, g_recv, tr_send, tr_recv, ts_send, ts_recv, ta_send, ta_recv,
             mr_send, ml_send, mf_send, m_recv, out_sem,
             a_buf, a_bf, a_in, bt, b_in, a_send, a_recv, b_send, b_recv):
    R, S, d, kv, rank = cfg
    L = R // 2
    me = lax.axis_index("replica")
    shard = lax.axis_index("shard")
    core = lax.rem(me, 2)
    pos = me // 2
    partner = me + 1 - 2 * core
    chunks = ld_sem.shape[1]
    rows = d // chunks

    def at_replica(r):
        return {"replica": r}

    def at_shard(s):
        return {"shard": s}

    loads = []
    for k in range(chunks):
        trio = []
        for n, (src, dst) in enumerate(((lw, lw_v), (base, base_v), (ef, ef_v))):
            part = pl.ds(k * rows, rows)
            cp = pltpu.make_async_copy(src.at[part], dst.at[part], ld_sem.at[n, k])
            cp.start()
            trio.append(cp)
        loads.append(trio)
    own_in = pltpu.make_async_copy(mom, slots.at[me], mom_ld.at[0])
    own_in.start()
    tok_in = pltpu.make_async_copy(tok, tok_v, mom_ld.at[1])
    tok_in.start()

    barrier = pltpu.get_barrier_semaphore()
    for k in range(1, R):
        pl.semaphore_signal(barrier, inc=1, device_id=at_replica(lax.rem(me + k, R)), device_id_type=MESH)
    for k in range(1, S):
        pl.semaphore_signal(barrier, inc=1, device_id=at_shard(lax.rem(shard + k, S)), device_id_type=MESH)
    pl.semaphore_wait(barrier, R - 1 + S - 1)

    def rcopy(src, dst, ss, rs, dev):
        return pltpu.make_async_remote_copy(src_ref=src, dst_ref=dst, send_sem=ss, recv_sem=rs,
                                            device_id=dev, device_id_type=MESH)

    def block_of(p):
        return 2 * p + core

    HV = 2
    span = d // HV

    def slot(b, hv):
        return slots.at[b, :, pl.ds(hv * span, span)]

    def move(step, hv, wait):
        right_origin = jnp.clip(pos - (step - 1), 0, L - 1)
        left_origin = jnp.clip(pos + (step - 1), 0, L - 1)

        def go(origin, sem, target):
            b = block_of(origin)
            cp = rcopy(slot(b, hv), slot(b, hv), sem.at[step - 1, hv], m_recv.at[b, hv], at_replica(block_of(target)))
            cp.wait_send() if wait else cp.start()

        @pl.when((pos - (step - 1) >= 0) & (pos + 1 < L))
        def _():
            go(right_origin, mr_send, jnp.minimum(pos + 1, L - 1))

        @pl.when((pos + (step - 1) < L) & (pos >= 1))
        def _():
            go(left_origin, ml_send, jnp.maximum(pos - 1, 0))

    def forward(b, side, index, hv, wait):
        cp = rcopy(slot(b, hv), slot(b, hv), mf_send.at[side, index, hv], m_recv.at[b, hv], at_replica(partner))
        cp.wait_send() if wait else cp.start()

    def await_half(b, hv):
        rcopy(slot(b, hv), slot(b, hv), mf_send.at[0, 0, hv], m_recv.at[b, hv], at_replica(partner)).wait_recv()

    def arrived(step, hv):
        for side, sign in enumerate((-1, 1)):
            origin = pos + sign * step

            @pl.when((origin >= 0) & (origin < L))
            def _():
                b = block_of(jnp.clip(origin, 0, L - 1))
                await_half(b, hv)
                forward(b, side, step - 1, hv, False)

    own_in.wait()
    for hv in range(HV):
        move(1, hv, False)
        forward(me, 0, L - 1, hv, False)

    c = slots.shape[1]
    per = 128 // c
    blocks = kv // 128
    n = tok.shape[0] // S
    early = per == 2

    def token_rows(s):
        return pl.ds(pl.multiple_of(s * n, 128), n)

    def block_cols(bk):
        return pl.ds(pl.multiple_of(bk * 128, 128), 128)

    def a_copy(k, bk):
        target = lax.rem(shard + k, S)
        return rcopy(a_bf.at[token_rows(target), block_cols(bk)], a_in.at[shard, :, block_cols(bk)],
                     a_send.at[k, bk], a_recv.at[shard, bk], at_shard(target))

    def mom_copy(bk):
        return pltpu.make_async_copy(mom_rows.at[:, block_cols(bk)], mom_out.at[:, block_cols(bk)], out_sem.at[bk])

    def key_block(bk):
        cols = block_cols(bk)
        block = slots[pl.ds(bk * per, per)].reshape(128, d)
        a = a_buf[:, cols] - (outer_rate * outer_mu * outer_mu) * lax.dot_general(
            tok_v[...], block, NT, preferred_element_type=F32)
        a_buf[:, cols] = a
        a_bf[:, cols] = a.astype(BF16)
        for k in range(1, S):
            a_copy(k, bk).start()
        mom_rows[:, cols] = block.T
        mom_copy(bk).start()

    def advance(step, hv):
        if step < L:
            arrived(step, hv)
        if step + 1 < L:
            move(step + 1, hv, False)

    def partner_block(p):
        for hv in range(HV):
            await_half(2 * p + 1 - core, hv)

    def blocks_at(step):
        def side(i, carry):
            origin = pos + (2 * i - 1) * step

            @pl.when((origin >= 0) & (origin < L))
            def _():
                p = jnp.clip(origin, 0, L - 1)
                partner_block(p)
                if early:
                    key_block(p)

            return carry

        lax.fori_loop(0, 2, side, 0)

    q3 = stack3(qt[...])
    for k in range(chunks):
        for cp in loads[k]:
            cp.wait()
        part = pl.ds(k * rows, rows)
        acc = lax.dot_general(q3, base_v[part, :], NT, preferred_element_type=F32)
        acc -= lax.dot_general(q3, lw_v[part, :], NT, preferred_element_type=F32)
        acc += lax.dot_general(q3, ef_v[part, :], NT, preferred_element_type=F32)
        pt[:, part] = fold3(acc)

    h = d // 2
    nc = L
    while h % nc or (h // nc) % 128:
        nc //= 2
    w = h // nc
    theirs = pl.ds(pl.multiple_of((1 - core) * h, 128), h)
    mine = pl.ds(pl.multiple_of(core * h, 128), h)
    pair = rcopy(pt.at[:, theirs], pair_in, pair_sem.at[0], pair_sem.at[1], at_replica(partner))
    pair.start()
    tok_in.wait()
    a_buf[...] = jnp.dot(tok_v[...], base_v[...], preferred_element_type=F32)
    pair.wait_recv()
    half[...] = pt[:, mine] + pair_in[...]

    owner = pos < nc

    def when_owner(f):
        if nc == L:
            f()
        else:
            pl.when(owner)(f)

    def rs_copy(k):
        target = lax.rem(pos + k, L)
        src = half.at[:, pl.ds(pl.multiple_of(jnp.minimum(target, nc - 1) * w, 128), w)]
        return target, rcopy(src, rs_in.at[pos], rs_send.at[k], rs_recv.at[pos], at_replica(block_of(target)))

    def per_target(k, f):
        target, cp = rs_copy(k)
        if nc == L:
            f(cp)
        else:
            pl.when(target < nc)(lambda: f(cp))

    for k in range(1, L):
        per_target(k, lambda cp: cp.start())
    partner_block(pos)
    if early:
        key_block(pos)
    advance(1, 0)
    own_pos = jnp.minimum(pos, nc - 1)

    def cols_of(c, p):
        return pl.ds(pl.multiple_of(c * h + p * w, 128), w)

    def reduce_own():
        total = half[:, pl.ds(pl.multiple_of(own_pos * w, 128), w)]
        for k in range(1, L):
            source = lax.rem(pos + k, L)
            rcopy(rs_in.at[source], rs_in.at[source], rs_send.at[k], rs_recv.at[source], at_replica(partner)).wait_recv()
            total += rs_in[source]
        pm[:, cols_of(core, own_pos)] = total * (1.0 / R)
        for k in range(1, L):
            ag_copy(k).start()
        fw_copy(core, own_pos, fw_send.at[0]).start()

    def ag_copy(k):
        dst = pm.at[:, cols_of(core, own_pos)]
        return rcopy(dst, dst, ag_send.at[k], ag_recv.at[core, own_pos], at_replica(block_of(lax.rem(pos + k, L))))

    def fw_copy(c, p, sem):
        dst = pm.at[:, cols_of(c, p)]
        return rcopy(dst, dst, sem, ag_recv.at[c, p], at_replica(partner))

    when_owner(reduce_own)
    for hv in range(1, HV):
        advance(1, hv)
    for k in range(1, L):
        source = lax.rem(pos + k, L)
        p = jnp.minimum(source, nc - 1)

        def take():
            fw_copy(core, p, fw_send.at[k]).wait_recv()
            fw_copy(core, p, fw_send.at[k]).start()

        if nc == L:
            take()
        else:
            pl.when(source < nc)(take)
    for p in range(nc):
        fw_copy(1 - core, p, fw_send.at[0]).wait_recv()

    acc = None
    for k in range(chunks):
        part = pl.ds(k * rows, rows)
        p3 = stack3(pm[:, part])
        term = lax.dot_general(p3, base_v[part, :], NN, preferred_element_type=F32)
        term -= lax.dot_general(p3, lw_v[part, :], NN, preferred_element_type=F32)
        term += lax.dot_general(p3, ef_v[part, :], NN, preferred_element_type=F32)
        acc = term if acc is None else acc + term
    tl[...] = fold3(acc)

    groups = rank // 8
    tiles = min(R, groups * (kv // 128))
    wl = kv // (tiles // groups)

    def tile_of(j):
        return (pl.ds(pl.multiple_of(lax.rem(j, groups) * 8, 8), 8),
                pl.ds(pl.multiple_of((j // groups) * wl, 128), wl))

    t_owner = me < tiles

    def when_tile(cond, f):
        if tiles == R:
            f()
        else:
            pl.when(cond)(f)

    def tr_copy(k):
        target = lax.rem(me + k, R)
        a, b = tile_of(jnp.minimum(target, tiles - 1))
        return target < tiles, rcopy(tl.at[a, b], tr_in.at[me], tr_send.at[k], tr_recv.at[me], at_replica(target))

    for k in range(1, R):
        cond, cp = tr_copy(k)
        when_tile(cond, lambda cp=cp: cp.start())

    advance(2, 0)

    whole_pm = pm[...]
    gs[...] = jnp.zeros_like(gs)
    gs[:, 0:rank] = lax.dot_general(whole_pm, whole_pm, NT, precision=HIGHEST, preferred_element_type=F32)

    def g_copy(k):
        return rcopy(gs, g_in.at[shard], g_send.at[k], g_recv.at[shard], at_shard(lax.rem(shard + k, S)))

    for k in range(1, S):
        g_copy(k).start()
    b_acc = None
    for k in range(chunks):
        part = pl.ds(k * rows, rows)
        term = lax.dot_general(stack3(pm[:, part]), tok_v[:, part], NT, preferred_element_type=F32)
        b_acc = term if b_acc is None else b_acc + term
    bt[...] = fold3(b_acc)

    def b_copy(k):
        target = lax.rem(shard + k, S)
        return rcopy(bt.at[:, token_rows(target)], b_in.at[shard], b_send.at[k], b_recv.at[shard], at_shard(target))

    for k in range(1, S):
        b_copy(k).start()

    my_tile = tile_of(jnp.minimum(me, tiles - 1))

    def ts_copy(k):
        return rcopy(ts, ts_in.at[shard], ts_send.at[k], ts_recv.at[shard], at_shard(lax.rem(shard + k, S)))

    def ta_copy(k):
        dst = tt.at[my_tile[0], my_tile[1]]
        return rcopy(dst, dst, ta_send.at[k], ta_recv.at[jnp.minimum(me, tiles - 1)], at_replica(lax.rem(me + k, R)))

    def reduce_replicas():
        total = tl[my_tile[0], my_tile[1]]
        for k in range(1, R):
            source = lax.rem(me + k, R)
            rcopy(tr_in.at[source], tr_in.at[source], tr_send.at[k], tr_recv.at[source], at_replica(partner)).wait_recv()
            total += tr_in[source]
        ts[...] = total
        for k in range(1, S):
            ts_copy(k).start()

    def reduce_shards():
        total = ts[...]
        for k in range(1, S):
            source = lax.rem(shard + k, S)
            rcopy(ts_in.at[source], ts_in.at[source], ts_send.at[k], ts_recv.at[source], at_replica(partner)).wait_recv()
            total += ts_in[source]
        tt[my_tile[0], my_tile[1]] = total * (1.0 / R)
        for k in range(1, R):
            ta_copy(k).start()

    when_tile(t_owner, reduce_replicas)
    for hv in range(1, HV):
        advance(2, hv)
    if L > 1:
        blocks_at(1)
    when_tile(t_owner, reduce_shards)

    if 2 < L - 1:
        blocks_at(2)

    gram = gs[:, 0:rank]
    for k in range(1, S):
        source = lax.rem(shard + k, S)
        rcopy(g_in.at[source], g_in.at[source], g_send.at[k], g_recv.at[source], at_replica(partner)).wait_recv()
        gram = gram + g_in[source][:, 0:rank]
    inverse = invert(gram)
    for step in range(3, L):
        for hv in range(HV):
            advance(step, hv)
        if step < L - 1:
            blocks_at(step)

    for k in range(1, R):
        source = lax.rem(me + k, R)
        j = jnp.minimum(source, tiles - 1)
        a, b = tile_of(j)

        def got(j=j, a=a, b=b, k=k):
            rcopy(tt.at[a, b], tt.at[a, b], ta_send.at[k], ta_recv.at[j], at_replica(partner)).wait_recv()

        when_tile(source < tiles, got)
    x = lax.dot_general(inverse, tt[...], NN, precision=HIGHEST, preferred_element_type=F32)
    x_out[...] = x
    own_columns = xo_out.shape[1]
    pick = (lax.broadcasted_iota(jnp.int32, (kv, own_columns), 0)
            == me * own_columns + lax.broadcasted_iota(jnp.int32, (kv, own_columns), 1)).astype(F32)
    xo_out[...] = lax.dot_general(x, pick, NN, precision=HIGHEST, preferred_element_type=F32)
    pm_out[...] = pm[...]

    if L > 2:
        blocks_at(L - 1)
    if not early:
        def late(bk, carry):
            key_block(bk)
            return carry

        lax.fori_loop(0, blocks, late, 0)

    total = a_buf[token_rows(shard), :]
    b_total = bt[:, token_rows(shard)]
    for k in range(1, S):
        source = lax.rem(shard + k, S)
        for bk in range(blocks):
            part = a_in.at[source, :, block_cols(bk)]
            rcopy(part, part, a_send.at[k, bk], a_recv.at[source, bk], at_replica(partner)).wait_recv()
        total += a_in[source].astype(F32)
        rcopy(b_in.at[source], b_in.at[source], b_send.at[k], b_recv.at[source], at_replica(partner)).wait_recv()
        b_total += b_in[source]
    a_out[...] = total
    b_out[...] = b_total
    for bk in range(blocks):
        mom_copy(bk).wait()

    for hv in range(HV):
        forward(me, 0, L - 1, hv, True)
    for k in range(1, S):
        for bk in range(blocks):
            a_copy(k, bk).wait_send()
        b_copy(k).wait_send()
    pair.wait_send()
    for k in range(1, L):
        per_target(k, lambda cp: cp.wait_send())

    def drain_own():
        for k in range(1, L):
            ag_copy(k).wait_send()
        fw_copy(core, own_pos, fw_send.at[0]).wait_send()

    when_owner(drain_own)
    for k in range(1, L):
        source = lax.rem(pos + k, L)
        p = jnp.minimum(source, nc - 1)

        def drain_fw(p=p, k=k):
            fw_copy(core, p, fw_send.at[k]).wait_send()

        if nc == L:
            drain_fw()
        else:
            pl.when(source < nc)(drain_fw)
    for k in range(1, S):
        g_copy(k).wait_send()
    for k in range(1, R):
        cond, cp = tr_copy(k)
        when_tile(cond, lambda cp=cp: cp.wait_send())

    def drain_tile():
        for k in range(1, S):
            ts_copy(k).wait_send()
        for k in range(1, R):
            ta_copy(k).wait_send()

    when_tile(t_owner, drain_tile)
    for step in range(1, L):
        for hv in range(HV):
            move(step, hv, True)
            for side, sign in enumerate((-1, 1)):
                origin = pos + sign * step

                @pl.when((origin >= 0) & (origin < L))
                def _():
                    forward(block_of(jnp.clip(origin, 0, L - 1)), side, step - 1, hv, True)


def local_step(tr, pm, x, xo, a_own, b_own, base, lw, ef, mom, mom_rows,
               nb_out, nm_out, ne_out, key_out, x6, xo6):
    step = pl.program_id(0)

    def six_x(v):
        a, b, l = split3(v)
        return jnp.concatenate([a, b, a, l, b, a], axis=0)

    @pl.when(step == 0)
    def _():
        x6[...] = six_x(x[...])
        xo6[...] = six_x(xo[...])
        key_out[...] = (a_own[...] - (outer_rate * (outer_mu + 1.0)) * lax.dot_general(
            b_own[...], x[...], TN, precision=HIGHEST, preferred_element_type=F32)).astype(BF16)

    a, b, l = split3(pm[...])
    p6 = jnp.concatenate([a, a, b, a, b, l], axis=0)
    update = lax.dot_general(p6, x6[...], TN, preferred_element_type=F32)
    own_update = lax.dot_general(xo6[...], p6, TN, preferred_element_type=F32)
    nm_out[...] = (outer_mu * mom[...].astype(F32) + own_update).astype(BF16)
    base32 = base[...].astype(F32)
    ne_out[...] = ((base32 - lw[...].astype(F32) + ef[...].astype(F32)) - update).astype(BF16)
    moment = outer_mu * mom_rows[...].astype(F32) + update
    nb_out[...] = (base32 - outer_rate * (outer_mu * moment + update)).astype(BF16)


def on_device(local_weights, outer_base, momentum, error_feedback, q_start, tokens):
    R = lax.axis_size("replica")
    S = lax.axis_size("shard")
    d, kv = outer_base.shape
    rank = q_start.shape[1]
    c = momentum.shape[1]
    L = R // 2
    lw, ef, tok = local_weights[0], error_feedback[0], tokens[0]
    nt = tok.shape[0]
    mom_t = momentum.T
    any_spec = pl.BlockSpec(memory_space=pl.ANY)
    vm = pl.BlockSpec(memory_space=pltpu.VMEM)
    chunks = min(4, d // 128)
    h = d // 2
    nc = L
    while h % nc or (h // nc) % 128:
        nc //= 2
    w = h // nc
    tiles = min(R, (rank // 8) * (kv // 128))
    wl = kv // (tiles // (rank // 8))
    V = pltpu.VMEM
    dma = pltpu.SemaphoreType.DMA
    n = nt // S
    pm, x, xo, a_own, b_own, mom_rows = pl.pallas_call(
        functools.partial(exchange, (R, S, d, kv, rank)),
        out_shape=(
            jax.ShapeDtypeStruct((rank, d), F32),
            jax.ShapeDtypeStruct((rank, kv), F32),
            jax.ShapeDtypeStruct((rank, c), F32),
            jax.ShapeDtypeStruct((n, kv), F32),
            jax.ShapeDtypeStruct((rank, n), F32),
            jax.ShapeDtypeStruct((d, kv), BF16),
        ),
        in_specs=[any_spec, any_spec, any_spec, vm, any_spec, any_spec],
        out_specs=(vm, vm, vm, vm, vm, any_spec),
        scratch_shapes=[
            V((d, kv), BF16), V((d, kv), BF16), V((d, kv), BF16), V((nt, d), BF16), V((R, c, d), BF16), V((d, kv), BF16),
            V((rank, d), F32), V((rank, h), F32), V((rank, h), F32), V((L, rank, w), F32), V((rank, d), F32),
            V((rank, 128), F32), V((S, rank, 128), F32),
            V((rank, kv), F32), V((R, 8, wl), F32), V((8, wl), F32), V((S, 8, wl), F32), V((rank, kv), F32),
            dma((3, chunks)), dma((2,)), dma((2,)), dma((L,)), dma((L,)), dma((L,)), dma((2, L)), dma((L,)),
            dma((S,)), dma((S,)), dma((R,)), dma((R,)), dma((S,)), dma((S,)), dma((R,)), dma((R,)),
            dma((L, 2)), dma((L, 2)), dma((2, L, 2)), dma((R, 2)), dma((kv // 128,)),
            V((nt, kv), F32), V((nt, kv), BF16), V((S, n, kv), BF16), V((rank, nt), F32), V((S, rank, n), F32),
            dma((S, kv // 128)), dma((S, kv // 128)), dma((S,)), dma((S,)),
        ],
        compiler_params=pltpu.CompilerParams(collective_id=0, has_side_effects=True),
        name="exchange",
    )(lw, outer_base, ef, q_start.T, mom_t, tok)

    tr = min(512, d)
    row = lambda i: (i, 0)
    nb, nm, ne, keys = pl.pallas_call(
        functools.partial(local_step, tr),
        grid=(d // tr,),
        out_shape=(
            jax.ShapeDtypeStruct((d, kv), BF16),
            jax.ShapeDtypeStruct((c, d), BF16),
            jax.ShapeDtypeStruct((d, kv), BF16),
            jax.ShapeDtypeStruct((n, kv), BF16),
        ),
        in_specs=[
            pl.BlockSpec((rank, tr), lambda i: (0, i)),
            pl.BlockSpec((rank, kv), lambda i: (0, 0)),
            pl.BlockSpec((rank, c), lambda i: (0, 0)),
            pl.BlockSpec((n, kv), lambda i: (0, 0)),
            pl.BlockSpec((rank, n), lambda i: (0, 0)),
            pl.BlockSpec((tr, kv), row),
            pl.BlockSpec((tr, kv), row),
            pl.BlockSpec((tr, kv), row),
            pl.BlockSpec((c, tr), lambda i: (0, i)),
            pl.BlockSpec((tr, kv), row),
        ],
        out_specs=(
            pl.BlockSpec((tr, kv), row),
            pl.BlockSpec((c, tr), lambda i: (0, i)),
            pl.BlockSpec((tr, kv), row),
            pl.BlockSpec((n, kv), lambda i: (0, 0)),
        ),
        scratch_shapes=[V((6 * rank, kv), BF16), V((6 * rank, c), BF16)],
        compiler_params=pltpu.CompilerParams(dimension_semantics=("arbitrary",)),
        name="local_step",
    )(pm, x, xo, a_own, b_own, outer_base, lw, ef, mom_t, mom_rows)

    return nb, nm.T, ne[None], keys[None]


def solution(mesh):
    in_specs = (
        P("replica", "shard", None),
        P("shard", None),
        P("shard", "replica"),
        P("replica", "shard", None),
        P(),
        P("replica", None, "shard"),
    )
    out_specs = (
        P("shard", None),
        P("shard", "replica"),
        P("replica", "shard", None),
        P("replica", "shard", None),
    )
    return jax.shard_map(
        on_device, mesh=mesh, in_specs=in_specs, out_specs=out_specs, check_vma=False
    )
```

```python
import functools

import jax
import jax.numpy as jnp
from jax import lax
from jax.experimental import pallas as pl
from jax.experimental.pallas import tpu as pltpu
from jax.sharding import PartitionSpec as P

outer_mu = 0.9
outer_rate = 0.7
MESH = pl.DeviceIdType.MESH
F32 = jnp.float32
BF16 = jnp.bfloat16
NT = (((1,), (1,)), ((), ()))
NN = (((1,), (0,)), ((), ()))
TN = (((0,), (0,)), ((), ()))
HIGHEST = lax.Precision.HIGHEST


def split3(x):
    high = x.astype(BF16)
    rest = x - high.astype(F32)
    mid = rest.astype(BF16)
    low = (rest - mid.astype(F32)).astype(BF16)
    return high, mid, low


def stack3(x):
    return jnp.concatenate(split3(x), axis=0)


def fold3(x):
    n = x.shape[0] // 3
    return x[:n] + (x[n : 2 * n] + x[2 * n :])


def invert(a):
    n = a.shape[0]
    rows = lax.broadcasted_iota(jnp.int32, (n, n), 0)
    cols = lax.broadcasted_iota(jnp.int32, (n, n), 1)
    lane = lax.broadcasted_iota(jnp.int32, (1, n), 1)
    for k in range(n):
        inverse_pivot = 1.0 / a[k : k + 1, k : k + 1]
        col = a[:, k : k + 1]
        row = jnp.where(lane == k, 1.0, a[k : k + 1, :]) * inverse_pivot
        a = jnp.where(rows == k, row, jnp.where(cols == k, 0.0, a) - col * row)
    return a


def exchange(cfg, lw, base, ef, qt, mom, tok, pm_out, x_out, xo_out, a_out, b_out, mom_out,
             lw_v, base_v, ef_v, tok_v, slots, mom_rows, pt, pair_in, half, rs_in, pm, gs, g_in,
             tl, tr_in, ts, ts_in, tt,
             ld_sem, mom_ld, pair_sem, rs_send, rs_recv, ag_send, ag_recv, fw_send,
             g_send, g_recv, tr_send, tr_recv, ts_send, ts_recv, ta_send, ta_recv,
             mr_send, ml_send, mf_send, m_recv, out_sem,
             a_buf, a_bf, a_in, bt, b_in, a_send, a_recv, b_send, b_recv):
    R, S, d, kv, rank = cfg
    L = R // 2
    me = lax.axis_index("replica")
    shard = lax.axis_index("shard")
    core = lax.rem(me, 2)
    pos = me // 2
    partner = me + 1 - 2 * core
    chunks = ld_sem.shape[1]
    rows = d // chunks

    def at_replica(r):
        return {"replica": r}

    def at_shard(s):
        return {"shard": s}

    loads = []
    for k in range(chunks):
        trio = []
        for n, (src, dst) in enumerate(((lw, lw_v), (base, base_v), (ef, ef_v))):
            part = pl.ds(k * rows, rows)
            cp = pltpu.make_async_copy(src.at[part], dst.at[part], ld_sem.at[n, k])
            cp.start()
            trio.append(cp)
        loads.append(trio)
    own_in = pltpu.make_async_copy(mom, slots.at[me], mom_ld.at[0])
    own_in.start()
    tok_in = pltpu.make_async_copy(tok, tok_v, mom_ld.at[1])
    tok_in.start()

    barrier = pltpu.get_barrier_semaphore()
    for k in range(1, R):
        pl.semaphore_signal(barrier, inc=1, device_id=at_replica(lax.rem(me + k, R)), device_id_type=MESH)
    for k in range(1, S):
        pl.semaphore_signal(barrier, inc=1, device_id=at_shard(lax.rem(shard + k, S)), device_id_type=MESH)
    pl.semaphore_wait(barrier, R - 1 + S - 1)

    def rcopy(src, dst, ss, rs, dev):
        return pltpu.make_async_remote_copy(src_ref=src, dst_ref=dst, send_sem=ss, recv_sem=rs,
                                            device_id=dev, device_id_type=MESH)

    def block_of(p):
        return 2 * p + core

    HV = 2
    span = d // HV

    def slot(b, hv):
        return slots.at[b, :, pl.ds(hv * span, span)]

    def move(step, hv, wait):
        right_origin = jnp.clip(pos - (step - 1), 0, L - 1)
        left_origin = jnp.clip(pos + (step - 1), 0, L - 1)

        def go(origin, sem, target):
            b = block_of(origin)
            cp = rcopy(slot(b, hv), slot(b, hv), sem.at[step - 1, hv], m_recv.at[b, hv], at_replica(block_of(target)))
            cp.wait_send() if wait else cp.start()

        @pl.when((pos - (step - 1) >= 0) & (pos + 1 < L))
        def _():
            go(right_origin, mr_send, jnp.minimum(pos + 1, L - 1))

        @pl.when((pos + (step - 1) < L) & (pos >= 1))
        def _():
            go(left_origin, ml_send, jnp.maximum(pos - 1, 0))

    def forward(b, side, index, hv, wait):
        cp = rcopy(slot(b, hv), slot(b, hv), mf_send.at[side, index, hv], m_recv.at[b, hv], at_replica(partner))
        cp.wait_send() if wait else cp.start()

    def await_half(b, hv):
        rcopy(slot(b, hv), slot(b, hv), mf_send.at[0, 0, hv], m_recv.at[b, hv], at_replica(partner)).wait_recv()

    def arrived(step, hv):
        for side, sign in enumerate((-1, 1)):
            origin = pos + sign * step

            @pl.when((origin >= 0) & (origin < L))
            def _():
                b = block_of(jnp.clip(origin, 0, L - 1))
                await_half(b, hv)
                forward(b, side, step - 1, hv, False)

    own_in.wait()
    for hv in range(HV):
        move(1, hv, False)
        forward(me, 0, L - 1, hv, False)

    c = slots.shape[1]
    per = 128 // c
    blocks = kv // 128
    n = tok.shape[0] // S
    early = per == 2

    def token_rows(s):
        return pl.ds(pl.multiple_of(s * n, 128), n)

    def block_cols(bk):
        return pl.ds(pl.multiple_of(bk * 128, 128), 128)

    def a_copy(k, bk):
        target = lax.rem(shard + k, S)
        return rcopy(a_bf.at[token_rows(target), block_cols(bk)], a_in.at[shard, :, block_cols(bk)],
                     a_send.at[k, bk], a_recv.at[shard, bk], at_shard(target))

    def mom_copy(bk):
        return pltpu.make_async_copy(mom_rows.at[:, block_cols(bk)], mom_out.at[:, block_cols(bk)], out_sem.at[bk])

    def key_block(bk):
        cols = block_cols(bk)
        block = slots[pl.ds(bk * per, per)].reshape(128, d)
        a = a_buf[:, cols] - (outer_rate * outer_mu * outer_mu) * lax.dot_general(
            tok_v[...], block, NT, preferred_element_type=F32)
        a_buf[:, cols] = a
        a_bf[:, cols] = a.astype(BF16)
        for k in range(1, S):
            a_copy(k, bk).start()
        mom_rows[:, cols] = block.T
        mom_copy(bk).start()

    def advance(step, hv):
        if step < L:
            arrived(step, hv)
        if step + 1 < L:
            move(step + 1, hv, False)

    def partner_block(p):
        for hv in range(HV):
            await_half(2 * p + 1 - core, hv)

    def blocks_at(step):
        def side(i, carry):
            origin = pos + (2 * i - 1) * step

            @pl.when((origin >= 0) & (origin < L))
            def _():
                p = jnp.clip(origin, 0, L - 1)
                partner_block(p)
                if early:
                    key_block(p)

            return carry

        lax.fori_loop(0, 2, side, 0)

    q3 = stack3(qt[...])
    for k in range(chunks):
        for cp in loads[k]:
            cp.wait()
        part = pl.ds(k * rows, rows)
        acc = lax.dot_general(q3, base_v[part, :], NT, preferred_element_type=F32)
        acc -= lax.dot_general(q3, lw_v[part, :], NT, preferred_element_type=F32)
        acc += lax.dot_general(q3, ef_v[part, :], NT, preferred_element_type=F32)
        pt[:, part] = fold3(acc)

    h = d // 2
    nc = L
    while h % nc or (h // nc) % 128:
        nc //= 2
    w = h // nc
    theirs = pl.ds(pl.multiple_of((1 - core) * h, 128), h)
    mine = pl.ds(pl.multiple_of(core * h, 128), h)
    pair = rcopy(pt.at[:, theirs], pair_in, pair_sem.at[0], pair_sem.at[1], at_replica(partner))
    pair.start()
    tok_in.wait()
    a_buf[...] = jnp.dot(tok_v[...], base_v[...], preferred_element_type=F32)
    pair.wait_recv()
    half[...] = pt[:, mine] + pair_in[...]

    owner = pos < nc

    def when_owner(f):
        if nc == L:
            f()
        else:
            pl.when(owner)(f)

    def rs_copy(k):
        target = lax.rem(pos + k, L)
        src = half.at[:, pl.ds(pl.multiple_of(jnp.minimum(target, nc - 1) * w, 128), w)]
        return target, rcopy(src, rs_in.at[pos], rs_send.at[k], rs_recv.at[pos], at_replica(block_of(target)))

    def per_target(k, f):
        target, cp = rs_copy(k)
        if nc == L:
            f(cp)
        else:
            pl.when(target < nc)(lambda: f(cp))

    for k in range(1, L):
        per_target(k, lambda cp: cp.start())
    partner_block(pos)
    if early:
        key_block(pos)
    advance(1, 0)
    own_pos = jnp.minimum(pos, nc - 1)

    def cols_of(c, p):
        return pl.ds(pl.multiple_of(c * h + p * w, 128), w)

    def reduce_own():
        total = half[:, pl.ds(pl.multiple_of(own_pos * w, 128), w)]
        for k in range(1, L):
            source = lax.rem(pos + k, L)
            rcopy(rs_in.at[source], rs_in.at[source], rs_send.at[k], rs_recv.at[source], at_replica(partner)).wait_recv()
            total += rs_in[source]
        pm[:, cols_of(core, own_pos)] = total * (1.0 / R)
        for k in range(1, L):
            ag_copy(k).start()
        fw_copy(core, own_pos, fw_send.at[0]).start()

    def ag_copy(k):
        dst = pm.at[:, cols_of(core, own_pos)]
        return rcopy(dst, dst, ag_send.at[k], ag_recv.at[core, own_pos], at_replica(block_of(lax.rem(pos + k, L))))

    def fw_copy(c, p, sem):
        dst = pm.at[:, cols_of(c, p)]
        return rcopy(dst, dst, sem, ag_recv.at[c, p], at_replica(partner))

    when_owner(reduce_own)
    for hv in range(1, HV):
        advance(1, hv)
    for k in range(1, L):
        source = lax.rem(pos + k, L)
        p = jnp.minimum(source, nc - 1)

        def take():
            fw_copy(core, p, fw_send.at[k]).wait_recv()
            fw_copy(core, p, fw_send.at[k]).start()

        if nc == L:
            take()
        else:
            pl.when(source < nc)(take)
    for p in range(nc):
        fw_copy(1 - core, p, fw_send.at[0]).wait_recv()

    acc = None
    for k in range(chunks):
        part = pl.ds(k * rows, rows)
        p3 = stack3(pm[:, part])
        term = lax.dot_general(p3, base_v[part, :], NN, preferred_element_type=F32)
        term -= lax.dot_general(p3, lw_v[part, :], NN, preferred_element_type=F32)
        term += lax.dot_general(p3, ef_v[part, :], NN, preferred_element_type=F32)
        acc = term if acc is None else acc + term
    tl[...] = fold3(acc)

    groups = rank // 8
    tiles = min(R, groups * (kv // 128))
    wl = kv // (tiles // groups)

    def tile_of(j):
        return (pl.ds(pl.multiple_of(lax.rem(j, groups) * 8, 8), 8),
                pl.ds(pl.multiple_of((j // groups) * wl, 128), wl))

    t_owner = me < tiles

    def when_tile(cond, f):
        if tiles == R:
            f()
        else:
            pl.when(cond)(f)

    def tr_copy(k):
        target = lax.rem(me + k, R)
        a, b = tile_of(jnp.minimum(target, tiles - 1))
        return target < tiles, rcopy(tl.at[a, b], tr_in.at[me], tr_send.at[k], tr_recv.at[me], at_replica(target))

    for k in range(1, R):
        cond, cp = tr_copy(k)
        when_tile(cond, lambda cp=cp: cp.start())

    advance(2, 0)

    whole_pm = pm[...]
    gs[...] = jnp.zeros_like(gs)
    gs[:, 0:rank] = lax.dot_general(whole_pm, whole_pm, NT, precision=HIGHEST, preferred_element_type=F32)

    def g_copy(k):
        return rcopy(gs, g_in.at[shard], g_send.at[k], g_recv.at[shard], at_shard(lax.rem(shard + k, S)))

    for k in range(1, S):
        g_copy(k).start()
    b_acc = None
    for k in range(chunks):
        part = pl.ds(k * rows, rows)
        term = lax.dot_general(stack3(pm[:, part]), tok_v[:, part], NT, preferred_element_type=F32)
        b_acc = term if b_acc is None else b_acc + term
    bt[...] = fold3(b_acc)

    def b_copy(k):
        target = lax.rem(shard + k, S)
        return rcopy(bt.at[:, token_rows(target)], b_in.at[shard], b_send.at[k], b_recv.at[shard], at_shard(target))

    for k in range(1, S):
        b_copy(k).start()

    my_tile = tile_of(jnp.minimum(me, tiles - 1))

    def ts_copy(k):
        return rcopy(ts, ts_in.at[shard], ts_send.at[k], ts_recv.at[shard], at_shard(lax.rem(shard + k, S)))

    def ta_copy(k):
        dst = tt.at[my_tile[0], my_tile[1]]
        return rcopy(dst, dst, ta_send.at[k], ta_recv.at[jnp.minimum(me, tiles - 1)], at_replica(lax.rem(me + k, R)))

    def reduce_replicas():
        total = tl[my_tile[0], my_tile[1]]
        for k in range(1, R):
            source = lax.rem(me + k, R)
            rcopy(tr_in.at[source], tr_in.at[source], tr_send.at[k], tr_recv.at[source], at_replica(partner)).wait_recv()
            total += tr_in[source]
        ts[...] = total
        for k in range(1, S):
            ts_copy(k).start()

    def reduce_shards():
        total = ts[...]
        for k in range(1, S):
            source = lax.rem(shard + k, S)
            rcopy(ts_in.at[source], ts_in.at[source], ts_send.at[k], ts_recv.at[source], at_replica(partner)).wait_recv()
            total += ts_in[source]
        tt[my_tile[0], my_tile[1]] = total * (1.0 / R)
        for k in range(1, R):
            ta_copy(k).start()

    when_tile(t_owner, reduce_replicas)
    for hv in range(1, HV):
        advance(2, hv)
    if L > 1:
        blocks_at(1)
    when_tile(t_owner, reduce_shards)

    if 2 < L - 1:
        blocks_at(2)

    gram = gs[:, 0:rank]
    for k in range(1, S):
        source = lax.rem(shard + k, S)
        rcopy(g_in.at[source], g_in.at[source], g_send.at[k], g_recv.at[source], at_replica(partner)).wait_recv()
        gram = gram + g_in[source][:, 0:rank]
    inverse = invert(gram)
    for step in range(3, L):
        for hv in range(HV):
            advance(step, hv)
        if step < L - 1:
            blocks_at(step)

    for k in range(1, R):
        source = lax.rem(me + k, R)
        j = jnp.minimum(source, tiles - 1)
        a, b = tile_of(j)

        def got(j=j, a=a, b=b, k=k):
            rcopy(tt.at[a, b], tt.at[a, b], ta_send.at[k], ta_recv.at[j], at_replica(partner)).wait_recv()

        when_tile(source < tiles, got)
    x = lax.dot_general(inverse, tt[...], NN, precision=HIGHEST, preferred_element_type=F32)
    x_out[...] = x
    own_columns = xo_out.shape[1]
    pick = (lax.broadcasted_iota(jnp.int32, (kv, own_columns), 0)
            == me * own_columns + lax.broadcasted_iota(jnp.int32, (kv, own_columns), 1)).astype(F32)
    xo_out[...] = lax.dot_general(x, pick, NN, precision=HIGHEST, preferred_element_type=F32)
    pm_out[...] = pm[...]

    if L > 2:
        blocks_at(L - 1)
    if not early:
        def late(bk, carry):
            key_block(bk)
            return carry

        lax.fori_loop(0, blocks, late, 0)

    total = a_buf[token_rows(shard), :]
    b_total = bt[:, token_rows(shard)]
    for k in range(1, S):
        source = lax.rem(shard + k, S)
        for bk in range(blocks):
            part = a_in.at[source, :, block_cols(bk)]
            rcopy(part, part, a_send.at[k, bk], a_recv.at[source, bk], at_replica(partner)).wait_recv()
        total += a_in[source].astype(F32)
        rcopy(b_in.at[source], b_in.at[source], b_send.at[k], b_recv.at[source], at_replica(partner)).wait_recv()
        b_total += b_in[source]
    a_out[...] = total
    b_out[...] = b_total
    for bk in range(blocks):
        mom_copy(bk).wait()

    for hv in range(HV):
        forward(me, 0, L - 1, hv, True)
    for k in range(1, S):
        for bk in range(blocks):
            a_copy(k, bk).wait_send()
        b_copy(k).wait_send()
    pair.wait_send()
    for k in range(1, L):
        per_target(k, lambda cp: cp.wait_send())

    def drain_own():
        for k in range(1, L):
            ag_copy(k).wait_send()
        fw_copy(core, own_pos, fw_send.at[0]).wait_send()

    when_owner(drain_own)
    for k in range(1, L):
        source = lax.rem(pos + k, L)
        p = jnp.minimum(source, nc - 1)

        def drain_fw(p=p, k=k):
            fw_copy(core, p, fw_send.at[k]).wait_send()

        if nc == L:
            drain_fw()
        else:
            pl.when(source < nc)(drain_fw)
    for k in range(1, S):
        g_copy(k).wait_send()
    for k in range(1, R):
        cond, cp = tr_copy(k)
        when_tile(cond, lambda cp=cp: cp.wait_send())

    def drain_tile():
        for k in range(1, S):
            ts_copy(k).wait_send()
        for k in range(1, R):
            ta_copy(k).wait_send()

    when_tile(t_owner, drain_tile)
    for step in range(1, L):
        for hv in range(HV):
            move(step, hv, True)
            for side, sign in enumerate((-1, 1)):
                origin = pos + sign * step

                @pl.when((origin >= 0) & (origin < L))
                def _():
                    forward(block_of(jnp.clip(origin, 0, L - 1)), side, step - 1, hv, True)


def local_step(tr, pm, x, xo, a_own, b_own, base, lw, ef, mom, mom_rows,
               nb_out, nm_out, ne_out, key_out, x6, xo6):
    step = pl.program_id(0)

    def six_x(v):
        a, b, l = split3(v)
        return jnp.concatenate([a, b, a, l, b, a], axis=0)

    @pl.when(step == 0)
    def _():
        x6[...] = six_x(x[...])
        xo6[...] = six_x(xo[...])
        key_out[...] = (a_own[...] - (outer_rate * (outer_mu + 1.0)) * lax.dot_general(
            b_own[...], x[...], TN, precision=HIGHEST, preferred_element_type=F32)).astype(BF16)

    a, b, l = split3(pm[...])
    p6 = jnp.concatenate([a, a, b, a, b, l], axis=0)
    update = lax.dot_general(p6, x6[...], TN, preferred_element_type=F32)
    own_update = lax.dot_general(xo6[...], p6, TN, preferred_element_type=F32)
    nm_out[...] = (outer_mu * mom[...].astype(F32) + own_update).astype(BF16)
    base32 = base[...].astype(F32)
    ne_out[...] = ((base32 - lw[...].astype(F32) + ef[...].astype(F32)) - update).astype(BF16)
    moment = outer_mu * mom_rows[...].astype(F32) + update
    nb_out[...] = (base32 - outer_rate * (outer_mu * moment + update)).astype(BF16)


def on_device(local_weights, outer_base, momentum, error_feedback, q_start, tokens):
    R = lax.axis_size("replica")
    S = lax.axis_size("shard")
    d, kv = outer_base.shape
    rank = q_start.shape[1]
    c = momentum.shape[1]
    L = R // 2
    lw, ef, tok = local_weights[0], error_feedback[0], tokens[0]
    nt = tok.shape[0]
    mom_t = momentum.T
    any_spec = pl.BlockSpec(memory_space=pl.ANY)
    vm = pl.BlockSpec(memory_space=pltpu.VMEM)
    chunks = min(4, d // 128)
    h = d // 2
    nc = L
    while h % nc or (h // nc) % 128:
        nc //= 2
    w = h // nc
    tiles = min(R, (rank // 8) * (kv // 128))
    wl = kv // (tiles // (rank // 8))
    V = pltpu.VMEM
    dma = pltpu.SemaphoreType.DMA
    n = nt // S
    pm, x, xo, a_own, b_own, mom_rows = pl.pallas_call(
        functools.partial(exchange, (R, S, d, kv, rank)),
        out_shape=(
            jax.ShapeDtypeStruct((rank, d), F32),
            jax.ShapeDtypeStruct((rank, kv), F32),
            jax.ShapeDtypeStruct((rank, c), F32),
            jax.ShapeDtypeStruct((n, kv), F32),
            jax.ShapeDtypeStruct((rank, n), F32),
            jax.ShapeDtypeStruct((d, kv), BF16),
        ),
        in_specs=[any_spec, any_spec, any_spec, vm, any_spec, any_spec],
        out_specs=(vm, vm, vm, vm, vm, any_spec),
        scratch_shapes=[
            V((d, kv), BF16), V((d, kv), BF16), V((d, kv), BF16), V((nt, d), BF16), V((R, c, d), BF16), V((d, kv), BF16),
            V((rank, d), F32), V((rank, h), F32), V((rank, h), F32), V((L, rank, w), F32), V((rank, d), F32),
            V((rank, 128), F32), V((S, rank, 128), F32),
            V((rank, kv), F32), V((R, 8, wl), F32), V((8, wl), F32), V((S, 8, wl), F32), V((rank, kv), F32),
            dma((3, chunks)), dma((2,)), dma((2,)), dma((L,)), dma((L,)), dma((L,)), dma((2, L)), dma((L,)),
            dma((S,)), dma((S,)), dma((R,)), dma((R,)), dma((S,)), dma((S,)), dma((R,)), dma((R,)),
            dma((L, 2)), dma((L, 2)), dma((2, L, 2)), dma((R, 2)), dma((kv // 128,)),
            V((nt, kv), F32), V((nt, kv), BF16), V((S, n, kv), BF16), V((rank, nt), F32), V((S, rank, n), F32),
            dma((S, kv // 128)), dma((S, kv // 128)), dma((S,)), dma((S,)),
        ],
        compiler_params=pltpu.CompilerParams(collective_id=0, has_side_effects=True),
        name="exchange",
    )(lw, outer_base, ef, q_start.T, mom_t, tok)

    tr = min(1024, d)
    row = lambda i: (i, 0)
    nb, nm, ne, keys = pl.pallas_call(
        functools.partial(local_step, tr),
        grid=(d // tr,),
        out_shape=(
            jax.ShapeDtypeStruct((d, kv), BF16),
            jax.ShapeDtypeStruct((c, d), BF16),
            jax.ShapeDtypeStruct((d, kv), BF16),
            jax.ShapeDtypeStruct((n, kv), BF16),
        ),
        in_specs=[
            pl.BlockSpec((rank, tr), lambda i: (0, i)),
            pl.BlockSpec((rank, kv), lambda i: (0, 0)),
            pl.BlockSpec((rank, c), lambda i: (0, 0)),
            pl.BlockSpec((n, kv), lambda i: (0, 0)),
            pl.BlockSpec((rank, n), lambda i: (0, 0)),
            pl.BlockSpec((tr, kv), row),
            pl.BlockSpec((tr, kv), row),
            pl.BlockSpec((tr, kv), row),
            pl.BlockSpec((c, tr), lambda i: (0, i)),
            pl.BlockSpec((tr, kv), row),
        ],
        out_specs=(
            pl.BlockSpec((tr, kv), row),
            pl.BlockSpec((c, tr), lambda i: (0, i)),
            pl.BlockSpec((tr, kv), row),
            pl.BlockSpec((n, kv), lambda i: (0, 0)),
        ),
        scratch_shapes=[V((6 * rank, kv), BF16), V((6 * rank, c), BF16)],
        compiler_params=pltpu.CompilerParams(dimension_semantics=("arbitrary",)),
        name="local_step",
    )(pm, x, xo, a_own, b_own, outer_base, lw, ef, mom_t, mom_rows)

    return nb, nm.T, ne[None], keys[None]


def solution(mesh):
    in_specs = (
        P("replica", "shard", None),
        P("shard", None),
        P("shard", "replica"),
        P("replica", "shard", None),
        P(),
        P("replica", None, "shard"),
    )
    out_specs = (
        P("shard", None),
        P("shard", "replica"),
        P("replica", "shard", None),
        P("replica", "shard", None),
    )
    return jax.shard_map(
        on_device, mesh=mesh, in_specs=in_specs, out_specs=out_specs, check_vma=False
    )
```
